32 devices in a mesh: teacher: 4 (over y, x), vocab: 8 (over z, core).
Axes of the slice: x: 2, y: 2, z: 4, core: 2. Of those that a mesh axis runs over, the one named last changes fastest.
Arguments:
- teacher_hidden: bfloat16 [4, 1024, 4096], P('teacher', 'vocab'), may hold values from -180 to 180
- teacher_head: bfloat16 [4, 4096, 32000], P('teacher', None, 'vocab'), may hold values from -0.375 to 0.375
- student_hidden: bfloat16 [1024, 4096], P('teacher'), may hold values from -180 to 180
- student_head: bfloat16 [4096, 32000], P('teacher', 'vocab'), may hold values from -0.375 to 0.375
Outputs:
- loss: float32 [], replicated
- grad_hidden: float32 [1024, 4096], P('teacher', 'vocab')
- grad_weight: float32 [4096, 32000], P('teacher', 'vocab')
The draws below stay inside these ranges and needn't reach their ends.
All inputs are finite; a program needn't handle non-finite values.
Results may differ from the reference program's by a relative error of at most 0.0027.
Values may be sent and summed in bfloat16 or wider, within the bound.
A program may use at most 192 MiB of HBM per device.

```python
import jax
import jax.numpy as jnp
from jax import lax

D = 4096
V = 32000
TOK = 1024
TEACHERS = 4


def rows_draw(key, shape):
    first = jax.random.fold_in(key, 0)
    values = jax.random.normal(first, shape, jnp.float32)
    return jnp.clip(values, -180.0, 180.0)


def draw_teacher_hidden(key, part):
    return rows_draw(jax.random.fold_in(key, 17), (TEACHERS, TOK, D)).astype(jnp.bfloat16)


def draw_student_hidden(key, part):
    return rows_draw(jax.random.fold_in(key, 29), (TOK, D)).astype(jnp.bfloat16)


def level_of(key, extent, cuts, low, top_value):
    level = 1.0
    for axis_at, parts in cuts:
        draws = jax.random.uniform(jax.random.fold_in(jax.random.fold_in(key, 6), axis_at), (parts,), jnp.float32, low / len(cuts), top_value / len(cuts))
        level = level * jnp.repeat(jnp.exp(draws), extent[axis_at] // parts).reshape((-1,) + (1,) * (len(extent) - 1 - axis_at))
    return level


def bell_draw(stream_key, shape, deviation, most, pieces=(), dtype=jnp.bfloat16):
    level = level_of(stream_key, shape, pieces, -0.22, 0.18) if pieces else 1.0
    entries = jax.random.normal(stream_key, shape, jnp.float32) * deviation * level
    return jnp.minimum(jnp.maximum(entries, -most), most).astype(dtype)


def setup_inputs(seed: int = 0) -> dict:
    streams_of = jax.random.split(jax.random.key(seed), 5)
    teacher_hidden = draw_teacher_hidden(jax.random.fold_in(streams_of[4], 71), 0)
    teacher_head = bell_draw(streams_of[1], (TEACHERS, D, V), (D // 16) ** -0.5, 0.375, ((0, 4), (2, 8)))
    student_hidden = draw_student_hidden(jax.random.fold_in(streams_of[4], 71), 0)
    student_head = bell_draw(streams_of[3], (D, V), (D // 16) ** -0.5, 0.375, ((0, 4), (1, 8)))
    return {"teacher_hidden": teacher_hidden, "teacher_head": teacher_head, "student_hidden": student_hidden, "student_head": student_head}


def row_stats(values):
    top = jnp.max(values, axis=-1, keepdims=True)
    shifted = jnp.exp(values - top)
    return top[..., 0], jnp.sum(shifted, axis=-1), jnp.sum(shifted * values, axis=-1)


def reference(teacher_hidden, teacher_head, student_hidden, student_head):
    def one_teacher(carry, pair):
        hidden, head = pair
        logits = jnp.dot(hidden, head, preferred_element_type=jnp.float32)
        top, total, moment = row_stats(logits)
        lse = top + jnp.log(total)
        entropy = lse - moment / total
        confid = jnp.exp(-entropy)
        return (carry[0] + confid[:, None] * (logits - lse[:, None]), carry[1] + confid), None

    init = (jnp.zeros((TOK, V), jnp.float32), jnp.zeros((TOK,), jnp.float32))
    (wsum, csum), _ = lax.scan(one_teacher, init, (teacher_hidden, teacher_head))
    raw = wsum / csum[:, None]
    top, total, _ = row_stats(raw)
    target = raw - (top + jnp.log(total))[:, None]
    slog = jnp.dot(student_hidden, student_head, preferred_element_type=jnp.float32)
    top, total, _ = row_stats(slog)
    slp = slog - (top + jnp.log(total))[:, None]
    probs = jnp.exp(target)
    loss = jnp.sum(probs * (target - slp)) / TOK
    gradl = (jnp.exp(slp) - probs).astype(jnp.bfloat16)
    grad_hidden = jnp.dot(gradl, student_head.T, preferred_element_type=jnp.float32)
    grad_weight = jnp.dot(student_hidden.T, gradl, preferred_element_type=jnp.float32)
    return loss, grad_hidden, grad_weight
```

```python
import functools

import jax
import jax.numpy as jnp
from jax import lax
from jax.experimental import pallas as pl
from jax.experimental.pallas import tpu as pltpu
from jax.sharding import PartitionSpec as P

F32 = jnp.float32
BF16 = jnp.bfloat16
MESH = pl.DeviceIdType.MESH
STEPS = 5
TURNS = 2 * STEPS
META = 16
OCT = 125.0
PIECES = 4
SLOTS = 5


def fold(x, op):
    return op(x.reshape(x.shape[0] // 8, 8, x.shape[1]), axis=0)


def level(top):
    return (top * 1.01 + 1e-30).astype(BF16).astype(F32)


def push(src, dst, ssem, rsem, **to):
    return pltpu.make_async_remote_copy(
        src_ref=src, dst_ref=dst, send_sem=ssem, recv_sem=rsem, device_id=to, device_id_type=MESH
    )


def square():
    t = lax.axis_index("teacher")
    return t, t + 1 - 2 * lax.rem(t, 2), lax.rem(t + 2, 4), 3 - t


def sub_rows(rows):
    for n in (80, 64, 48, 32, 16):
        if rows % n == 0:
            return n


class Halving:
    def __init__(self, bufs, part):
        self.s1, self.r1, self.s2, self.r2, self.ss1, self.sr1, self.ss2, self.sr2 = bufs
        self.part = part
        self.sub = sub_rows(part)
        self.t, self.px, self.py, self.across = square()

    def near(self, i):
        return jnp.where(lax.rem(i, 2) == 0, self.px, self.py)

    def far(self, i):
        return jnp.where(lax.rem(i, 2) == 0, self.py, self.px)

    def first(self, i):
        return push(self.s1.at[i], self.r1.at[i], self.ss1.at[i], self.sr1.at[i], teacher=self.near(i))

    def second(self, i):
        return push(self.s2.at[i], self.r2.at[i], self.ss2.at[i], self.sr2.at[i], teacher=self.far(i))

    def meta(self, reach, c):
        hi = c.astype(BF16).astype(F32)
        mid = (c - hi).astype(BF16).astype(F32)
        lo = c - hi - mid
        row = lax.broadcasted_iota(jnp.int32, (META, c.shape[1]), 0)
        rows = jnp.where(row == 0, reach, jnp.where(row == 1, hi, jnp.where(row == 2, mid, lo)))
        return rows.astype(BF16)

    def read_meta(self, ref):
        m = ref[pl.ds(self.part, META), :].astype(F32)
        return m[0:1], m[1:2] + m[2:3] + m[3:4]

    def loop(self, body):
        def one(j, carry):
            body(pl.ds(pl.multiple_of(j * self.sub, self.sub), self.sub))
            return carry

        lax.fori_loop(0, self.part // self.sub, one, 0)

    def send(self, i, value, top, weight):
        for b, owner in enumerate((self.near(i), self.across)):
            reach = level(top(i, owner))
            rate = OCT / reach
            dst = self.s1.at[i, b]

            def body(rows):
                dst[rows, :] = jnp.exp2(value(i, owner, rows) * rate).astype(BF16)

            self.loop(body)
            dst[pl.ds(self.part, META), :] = self.meta(reach, weight(owner))
        self.first(i).start()

    def relay(self, i, value, top, weight):
        self.first(i).wait_recv()
        owner = self.far(i)
        src = self.r1.at[i, 1]
        dst = self.s2.at[i]
        r, c = self.read_meta(src)
        reach = level(r + top(i, owner))
        rate = OCT / reach
        back = r * (1.0 / OCT)

        def body(rows):
            y = jnp.log2(src[rows, :].astype(F32)) * back
            dst[rows, :] = jnp.exp2((value(i, owner, rows) + y) * rate).astype(BF16)

        self.loop(body)
        dst[pl.ds(self.part, META), :] = self.meta(reach, c + weight(owner))
        self.second(i).start()

    def finish(self, i, value, weight, emit):
        self.second(i).wait_recv()
        one, two = self.r1.at[i, 0], self.r2.at[i]
        r1, c1 = self.read_meta(one)
        r2, c2 = self.read_meta(two)
        k1, k2 = r1 * (1.0 / OCT), r2 * (1.0 / OCT)
        total = c1 + c2 + weight(self.t)

        def body(rows):
            y = jnp.log2(one[rows, :].astype(F32)) * k1
            z = jnp.log2(two[rows, :].astype(F32)) * k2
            emit(i, rows, value(i, self.t, rows) + y + z, total)

        self.loop(body)

    def drain(self):
        def one(i, carry):
            self.first(i).wait_send()
            self.second(i).wait_send()
            return carry

        lax.fori_loop(0, TURNS, one, 0)


def halving_scratch(part, own):
    sem = pltpu.SemaphoreType.DMA((TURNS,))
    one, two = (TURNS, 2, part + META, own), (TURNS, part + META, own)
    return [pltpu.VMEM(one, BF16)] * 2 + [pltpu.VMEM(two, BF16)] * 2 + [sem] * 4


def turn_row(i, width, part):
    return lax.rem(i, 2) * (width // 2) + i // 2 * part


NT = (((1,), (1,)), ((), ()))


def forward_kernel(chips, th, head, sh, shead, logits, stat, slog, cols, *scratch):
    halving = Halving(scratch[:8], head.shape[0] // TURNS)
    (hid, wbuf, ws, work, tops, acc, wsem, lsem, outsem, zs, zr, cs, cr, os_, or_, fs, fr, gs, gr) = scratch[8:]
    width = head.shape[0]
    part = width // TURNS
    rows = th.shape[0]
    piece = rows // PIECES
    feats = ws.shape[1]
    own = sh.shape[0]
    hops = chips - 1
    tiles = TURNS
    t = halving.t
    v = lax.axis_index("vocab")
    core = lax.rem(v, 2)
    chip = v // 2
    twin = v + 1 - 2 * core
    others = (halving.px, halving.py, halving.across)

    barrier = pltpu.get_barrier_semaphore()
    for p in others:
        pl.semaphore_signal(barrier, inc=1, device_id={"teacher": p}, device_id_type=MESH)
    pl.semaphore_signal(barrier, inc=1, device_id={"vocab": twin}, device_id_type=MESH)

    @pl.when(chip > 0)
    def _():
        pl.semaphore_signal(barrier, inc=1, device_id={"vocab": v - 2}, device_id_type=MESH)

    @pl.when(chip < chips - 1)
    def _():
        pl.semaphore_signal(barrier, inc=1, device_id={"vocab": v + 2}, device_id_type=MESH)

    def tile_copy(g):
        slot = lax.rem(g, 2)
        at = pl.ds(pl.multiple_of(lax.rem(g, tiles) * part, part), part)
        return pltpu.make_async_copy(head.at[at], wbuf.at[slot], wsem.at[slot])

    def lanes(n):
        return pl.ds(pl.multiple_of(n * feats, feats), feats)

    def block(s, c):
        return pl.ds(pl.multiple_of((s * 2 + c) * rows, rows), rows)

    own_hid = pltpu.make_async_copy(th, hid.at[block(chip, core)], lsem.at[0])
    own_cols = pltpu.make_async_copy(sh.at[:, lanes(t)], cols.at[pl.ds(pl.multiple_of(t * own, own), own)], lsem.at[1])
    own_ws = pltpu.make_async_copy(shead, ws, lsem.at[2])
    own_hid.start()
    tile_copy(0).start()
    own_cols.start()
    own_ws.start()

    @pl.when((chip > 0) & (chip < chips - 1))
    def _():
        pl.semaphore_wait(barrier, 6)

    @pl.when((chip == 0) | (chip == chips - 1))
    def _():
        pl.semaphore_wait(barrier, 5)

    half = own // 2

    def col_rows(owner):
        return pl.ds(pl.multiple_of(owner * own + core * half, half), half)

    def col_out(n):
        src = sh.at[pl.ds(pl.multiple_of(core * half, half), half), lanes(others[n])]
        return push(src, cols.at[col_rows(t)], fs.at[n], fr.at[n], teacher=others[n])

    def col_twin(n):
        at = cols.at[col_rows(others[n])]
        return push(at, at, gs.at[n], gr.at[n], vocab=twin)

    for n in range(3):
        col_out(n).start()

    twin_own = push(th, hid.at[block(chip, core)], os_.at[0], or_.at[0], vocab=twin)
    twin_own.start()

    def at(s, q):
        return hid.at[pl.ds(pl.multiple_of((s * 2 + core) * rows + q * piece, piece), piece)]

    def along(d, h, q):
        s = chip - h if d == 0 else chip + h
        return push(at(s, q), at(s, q), zs.at[d, h, q], zr.at[d, h, q], vocab=v + 2 if d == 0 else v - 2)

    def arrived(d, h, q):
        s = chip - 1 - h if d == 0 else chip + 1 + h
        return push(at(s, q), at(s, q), zs.at[d, h, q], zr.at[d, h, q], vocab=v + 2 if d == 0 else v - 2)

    def across(d, h, q):
        s = chip - 1 - h if d == 0 else chip + 1 + h
        return push(at(s, q), at(s, q), cs.at[d, h, q], cr.at[d, h, q], vocab=twin)

    def arrives(d, h):
        return chip - 1 - h >= 0 if d == 0 else chip + 1 + h <= chips - 1

    def sends(d, h):
        return (chip - h >= 0) & (chip + 1 <= chips - 1) if d == 0 else (chip + h <= chips - 1) & (chip >= 1)

    own_hid.wait()
    for d in range(2):

        @pl.when(sends(d, 0))
        def _():
            for q in range(PIECES):
                along(d, 0, q).start()

    def event(j, carry):
        h = j // PIECES
        q = lax.rem(j, PIECES)
        for d in range(2):

            @pl.when(arrives(d, h))
            def _():
                arrived(d, h, q).wait_recv()
                across(d, h, q).start()

            @pl.when(arrives(d, h) & sends(d, h + 1))
            def _():
                along(d, h + 1, q).start()

        return carry

    short = jnp.minimum(chip, chips - 1 - chip)

    def source(p):
        d = (p + 1) // 2
        near = jnp.where(lax.rem(p, 2) == 1, chip - d, chip + d)
        beyond = jnp.where(chip == short, chip + p - short, chip - p + short)
        return jnp.where(p <= 2 * short, near, beyond)

    def flush(s):
        return pltpu.make_async_copy(acc, logits.at[s], outsem.at[0])

    def tile(g, carry):
        p = g // tiles
        kt = lax.rem(g, tiles)
        s = source(p)

        @pl.when(g + 1 < chips * tiles)
        def _():
            tile_copy(g + 1).start()

        @pl.when(kt == 0)
        def _():
            @pl.when(p == 0)
            def _():
                twin_own.wait_recv()

            for d in range(2):

                @pl.when((s < chip) if d == 0 else (s > chip))
                def _():
                    h = (chip - s if d == 0 else s - chip) - 1
                    for q in range(PIECES):
                        across(d, h, q).wait_recv()

            @pl.when(p > 0)
            def _():
                flush(0).wait()

        tile_copy(g).wait()
        a = hid[pl.ds(pl.multiple_of(s * 2 * rows, 2 * rows), 2 * rows), :]
        acc[pl.ds(pl.multiple_of(kt * part, part), part), :] = lax.dot_general(
            wbuf[lax.rem(g, 2)], a, NT, preferred_element_type=F32
        )

        @pl.when(kt == tiles - 1)
        def _():
            flush(s).start()
            sub = halving.sub
            n = 2 * rows

            def ends(j, c):
                x = acc[pl.ds(pl.multiple_of(j * sub, sub), sub), :]
                return jnp.maximum(c[0], fold(x, jnp.max)), jnp.minimum(c[1], fold(x, jnp.min))

            big = jnp.full((8, n), 3e38, F32)
            hi, low = lax.fori_loop(0, width // sub, ends, (-big, big))
            m = jnp.max(hi, axis=0, keepdims=True)

            def sums(j, c):
                x = acc[pl.ds(pl.multiple_of(j * sub, sub), sub), :]
                e = jnp.exp(x - m)
                return c[0] + fold(e, jnp.sum), c[1] + fold(e * x, jnp.sum)

            zero = jnp.zeros((8, n), F32)
            z, f = lax.fori_loop(0, width // sub, sums, (zero, zero))
            z, f = jnp.sum(z, axis=0, keepdims=True), jnp.sum(f, axis=0, keepdims=True)
            low = jnp.min(low, axis=0, keepdims=True)
            row = lax.broadcasted_iota(jnp.int32, (8, n), 0)
            stat[s] = jnp.where(row == 0, m, jnp.where(row == 1, z, jnp.where(row == 2, f, low)))

        return carry

    lax.fori_loop(0, tiles - 2, tile, 0)
    for n in range(3):
        col_out(n).wait_recv()
        col_twin(n).start()
    lax.fori_loop(tiles - 2, tiles, tile, 0)
    for n in range(3):
        col_twin(n).wait_recv()
    own_cols.wait()
    own_ws.wait()

    def value(i, owner, r):
        return work[lax.rem(i, SLOTS), owner, r, :]

    def top(i, owner):
        return jnp.max(tops[lax.rem(i, SLOTS), owner], axis=0, keepdims=True)

    def weight(owner):
        return jnp.ones((1, own), F32)

    def emit(i, r, x, c):
        slog[pl.ds(pl.multiple_of(turn_row(i, width, part) + r.start, halving.sub), halving.sub), :] = x

    events = hops * PIECES

    def seen(i):
        return jnp.where(i < 0, 0, jnp.minimum(2 + 6 * jnp.maximum(i, 0) // 5, events))

    def done(i):
        one = jnp.minimum(tiles + 4 * jnp.maximum(i - 1, 0), 2 * tiles)
        two = jnp.minimum(2 * tiles + 3 * jnp.maximum(i - 4, 0), 3 * tiles)
        three = jnp.minimum(3 * tiles + 4 * jnp.maximum(i - 8, 0), 4 * tiles)
        return jnp.where(i < 5, one, jnp.where(i < 9, two, three))

    def turn(i, carry):
        lax.fori_loop(seen(i - 1), seen(i), event, 0)

        @pl.when(i < TURNS)
        def _():
            a = ws[pl.ds(pl.multiple_of(turn_row(i, width, part), META), part), :]
            for owner in range(4):
                x = lax.dot_general(a, cols[pl.ds(owner * own, own), :], NT, preferred_element_type=F32)
                work[lax.rem(i, SLOTS), owner] = x
                tops[lax.rem(i, SLOTS), owner] = fold(jnp.abs(x), jnp.max)
            halving.send(i, value, top, weight)

        @pl.when((i >= 2) & (i < TURNS + 2))
        def _():
            halving.relay(i - 2, value, top, weight)

        @pl.when(i >= 4)
        def _():
            halving.finish(i - 4, value, weight, emit)

        lax.fori_loop(done(i - 1), done(i), tile, 0)
        return carry

    lax.fori_loop(0, TURNS + 4, turn, 0)

    flush(0).wait()
    halving.drain()
    for n in range(3):
        col_out(n).wait_send()
        col_twin(n).wait_send()
    twin_own.wait_send()

    def sent(j, carry):
        h = j // PIECES
        q = lax.rem(j, PIECES)
        for d in range(2):

            @pl.when(sends(d, h))
            def _():
                along(d, h, q).wait_send()

            @pl.when(arrives(d, h))
            def _():
                across(d, h, q).wait_send()

        return carry

    lax.fori_loop(0, events, sent, 0)


def forward(th, head, sh, shead, nv, ident):
    chips = nv // 2
    rows, depth = th.shape
    width = head.shape[0]
    feats = shead.shape[1]
    own = sh.shape[0]
    part = width // TURNS
    hops = chips - 1
    hbm = pl.BlockSpec(memory_space=pl.ANY)
    vmem = pl.BlockSpec(memory_space=pltpu.VMEM)
    dma = pltpu.SemaphoreType.DMA
    relays = dma((2, hops, PIECES))
    return pl.pallas_call(
        functools.partial(forward_kernel, chips),
        out_shape=(
            jax.ShapeDtypeStruct((chips, width, 2 * rows), F32),
            jax.ShapeDtypeStruct((chips, 8, 2 * rows), F32),
            jax.ShapeDtypeStruct((width, own), F32),
            jax.ShapeDtypeStruct((4 * own, feats), BF16),
        ),
        in_specs=[hbm] * 4,
        out_specs=(hbm, vmem, vmem, vmem),
        scratch_shapes=halving_scratch(part, own)
        + [
            pltpu.VMEM((nv * rows, depth), BF16),
            pltpu.VMEM((2, part, depth), BF16),
            pltpu.VMEM((width, feats), BF16),
            pltpu.VMEM((SLOTS, 4, part, own), F32),
            pltpu.VMEM((SLOTS, 4, 8, own), F32),
            pltpu.VMEM((width, 2 * rows), F32),
            dma((2,)),
            dma((3,)),
            dma((1,)),
            relays,
            relays,
            relays,
            relays,
            dma((1,)),
            dma((1,)),
            dma((3,)),
            dma((3,)),
            dma((3,)),
            dma((3,)),
        ],
        compiler_params=pltpu.CompilerParams(
            collective_id=ident, has_side_effects=True, vmem_limit_bytes=60 * 2**20
        ),
        name="forward",
    )(th, head, sh, shead)


def combine_kernel(nv, logits, stat, slog, grad, kl, *scratch):
    width, own = slog.shape
    part = width // TURNS
    halving = Halving(scratch[:8], part)
    lg, raw, peak, st, mine, st2, lsem, ssem, rsem, ssem2, rsem2 = scratch[8:]
    t = halving.t
    v = lax.axis_index("vocab")
    sub = halving.sub

    def fetch(n, owner):
        return pltpu.make_async_copy(logits.at[owner], lg.at[owner], lsem.at[n])

    order = (halving.px, halving.across, halving.py, t)
    for n in range(4):
        fetch(n, order[n]).start()

    barrier = pltpu.get_barrier_semaphore()
    for p in (halving.px, halving.py):
        pl.semaphore_signal(barrier, inc=1, device_id={"teacher": p}, device_id_type=MESH)
    for n in range(1, nv):
        pl.semaphore_signal(barrier, inc=1, device_id={"vocab": lax.rem(v + n, nv)}, device_id_type=MESH)
    pl.semaphore_wait(barrier, nv + 1)

    def share(n, src, dst, ss, rs):
        return push(src, dst.at[v], ss.at[n - 1], rs.at[n - 1], vocab=lax.rem(v + n, nv))

    for n in range(1, nv):
        share(n, stat, st, ssem, rsem).start()
    st[v] = stat[...]

    zero = jnp.zeros((8, own), F32)

    def at(j):
        return pl.ds(pl.multiple_of(j * sub, sub), sub)

    ms = jnp.max(
        lax.fori_loop(0, width // sub, lambda j, c: jnp.maximum(c, fold(slog[at(j), :], jnp.max)), zero - 3e38),
        axis=0,
        keepdims=True,
    )
    ss = jnp.sum(
        lax.fori_loop(0, width // sub, lambda j, c: c + fold(jnp.exp(slog[at(j), :] - ms), jnp.sum), zero),
        axis=0,
        keepdims=True,
    )
    for n in range(1, nv):
        share(n, stat, st, ssem, rsem).wait()

    for o in range(4):
        m = [st[s, o, 0:1, :] for s in range(nv)]
        big = functools.reduce(jnp.maximum, m)
        scale = [jnp.exp(x - big) for x in m]
        total = sum(st[s, o, 1:2, :] * scale[s] for s in range(nv))
        moment = sum(st[s, o, 2:3, :] * scale[s] for s in range(nv))
        lse = big + jnp.log(total)
        conf = jnp.exp(moment / total - lse)
        reach = conf * jnp.maximum(jnp.abs(stat[o, 0:1, :] - lse), jnp.abs(stat[o, 3:4, :] - lse))
        row = lax.broadcasted_iota(jnp.int32, (8, own), 0)
        mine[o] = jnp.where(row == 0, conf, jnp.where(row == 1, lse, reach))
    for n in range(4):
        fetch(n, order[n]).wait()

    def value(i, owner, r):
        rows = pl.ds(pl.multiple_of(turn_row(i, width, part) + r.start, sub), sub)
        return mine[owner, 0:1, :] * (lg[owner, rows, :] - mine[owner, 1:2, :])

    def top(i, owner):
        return mine[owner, 2:3, :]

    def weight(owner):
        return mine[owner, 0:1, :]

    peak[...] = zero - 3e38

    def emit(i, r, x, c):
        rows = pl.ds(pl.multiple_of(turn_row(i, width, part) + r.start, sub), sub)
        x = x * (1.0 / c)
        raw[rows, :] = x
        peak[...] = jnp.maximum(peak[...], fold(x, jnp.max))

    def turn(i, carry):
        @pl.when(i < TURNS)
        def _():
            halving.send(i, value, top, weight)

        @pl.when((i >= 2) & (i < TURNS + 2))
        def _():
            halving.relay(i - 2, value, top, weight)

        @pl.when(i >= 4)
        def _():
            halving.finish(i - 4, value, weight, emit)

        return carry

    lax.fori_loop(0, TURNS + 4, turn, 0)

    mr = jnp.max(peak[...], axis=0, keepdims=True)

    def sums(j, c):
        x = raw[at(j), :]
        e = jnp.exp(x - mr)
        return c[0] + fold(e, jnp.sum), c[1] + fold(e * (x - slog[at(j), :]), jnp.sum)

    sr, cross = lax.fori_loop(0, width // sub, sums, (zero, zero))
    sr, cross = jnp.sum(sr, axis=0, keepdims=True), jnp.sum(cross, axis=0, keepdims=True)
    row = lax.broadcasted_iota(jnp.int32, (8, own), 0)
    mine[0] = jnp.where(
        row == 0, mr, jnp.where(row == 1, sr, jnp.where(row == 2, cross, jnp.where(row == 3, ms, ss)))
    )
    for n in range(1, nv):
        share(n, mine.at[0], st2, ssem2, rsem2).start()
    st2[v] = mine[0]
    halving.drain()
    for n in range(1, nv):
        share(n, mine.at[0], st2, ssem2, rsem2).wait()
    every = [st2[s] for s in range(nv)]
    tr = functools.reduce(jnp.maximum, [x[0:1] for x in every])
    ts = functools.reduce(jnp.maximum, [x[3:4] for x in every])
    cr = [jnp.exp(x[0:1] - tr) for x in every]
    total_r = sum(x[1:2] * c for x, c in zip(every, cr))
    cross = sum(x[2:3] * c for x, c in zip(every, cr))
    total_s = sum(x[4:5] * jnp.exp(x[3:4] - ts) for x in every)
    lse_r = tr + jnp.log(total_r)
    lse_s = ts + jnp.log(total_s)
    kl[...] = jnp.broadcast_to(cross / total_r - lse_r + lse_s, (8, own))

    def grads(j, c):
        grad[at(j), :] = (jnp.exp(slog[at(j), :] - lse_s) - jnp.exp(raw[at(j), :] - lse_r)).astype(BF16)
        return c

    lax.fori_loop(0, width // sub, grads, 0)


def combine(logits, stat, slog, nv, ident):
    width, own = slog.shape
    part = width // TURNS
    hbm = pl.BlockSpec(memory_space=pl.ANY)
    vmem = pl.BlockSpec(memory_space=pltpu.VMEM)
    dma = pltpu.SemaphoreType.DMA
    return pl.pallas_call(
        functools.partial(combine_kernel, nv),
        out_shape=(jax.ShapeDtypeStruct((width, own), BF16), jax.ShapeDtypeStruct((8, own), F32)),
        in_specs=[hbm, vmem, vmem],
        out_specs=(vmem, vmem),
        scratch_shapes=halving_scratch(part, own)
        + [
            pltpu.VMEM((4, width, own), F32),
            pltpu.VMEM((width, own), F32),
            pltpu.VMEM((8, own), F32),
            pltpu.VMEM((nv, 4, 8, own), F32),
            pltpu.VMEM((4, 8, own), F32),
            pltpu.VMEM((nv, 8, own), F32),
            dma((4,)),
            dma((nv - 1,)),
            dma((nv - 1,)),
            dma((nv - 1,)),
            dma((nv - 1,)),
        ],
        compiler_params=pltpu.CompilerParams(
            collective_id=ident, has_side_effects=True, vmem_limit_bytes=60 * 2**20
        ),
        name="combine",
    )(logits, stat, slog)


def spread(nt, nv, gh, feats):
    r = nv // nt
    part = lax.rem(lax.axis_index("vocab"), r)
    rows, width = gh.shape[0], feats // r
    grad_hidden = jnp.zeros((r, rows, width), F32)
    for k in range(r):
        swap = [
            (s * nv + t * r + h, t * nv + s * r + (h + k) % r)
            for s in range(nt)
            for t in range(nt)
            for h in range(r)
        ]
        piece = lax.dynamic_slice(gh, (0, lax.rem(part + k, r) * width), (rows, width))
        piece = lax.ppermute(piece, ("teacher", "vocab"), swap)
        grad_hidden = lax.dynamic_update_slice(
            grad_hidden, piece[None], (lax.rem(part + r - k, r), 0, 0)
        )
    return grad_hidden.reshape(r * rows, width)


def gather_hidden(own, nv, first):
    chips = nv // 2
    at = lax.axis_index("vocab")
    chip = at // 2
    up = [own]
    down = [own]
    for hop in range(chips - 1):
        up.append(lax.ppermute(up[-1], "vocab", [(i, i + 2) for i in range(nv - 2)]))
        down.append(lax.ppermute(down[-1], "vocab", [(i + 2, i) for i in range(nv - 2)]))
        if hop == 1:
            up[-1], down[-1], first = lax.optimization_barrier((up[-1], down[-1], first))
    pair = [(i, i ^ 1) for i in range(nv)]
    rows, width = own.shape
    buf = jnp.zeros((chips, 2, rows, width), own.dtype)
    core = at % 2
    for k in range(chips):
        piece = own if k == 0 else up[k] + down[chips - k]
        other = lax.ppermute(piece, "vocab", pair)
        slot = lax.rem(chip - k + chips, chips)
        buf = lax.dynamic_update_slice(buf, piece[None, None], (slot, core, 0, 0))
        buf = lax.dynamic_update_slice(buf, other[None, None], (slot, 1 - core, 0, 0))
    return buf.reshape(nv * rows, width), first


def exchange_kernel(nv, own_ref, out_ref, slots, send, recv):
    me = lax.axis_index("vocab")
    barrier = pltpu.get_barrier_semaphore()
    for step in range(1, nv):
        pl.semaphore_signal(
            barrier,
            inc=1,
            device_id={"vocab": lax.rem(me + step, nv)},
            device_id_type=pl.DeviceIdType.MESH,
        )
    pl.semaphore_wait(barrier, nv - 1)
    copies = []
    for step in range(1, nv):
        copies.append(
            pltpu.make_async_remote_copy(
                src_ref=own_ref,
                dst_ref=slots.at[me],
                send_sem=send.at[step - 1],
                recv_sem=recv.at[step - 1],
                device_id={"vocab": lax.rem(me + step, nv)},
                device_id_type=pl.DeviceIdType.MESH,
            )
        )
        copies[-1].start()
    slots[me] = own_ref[...]
    for copy in copies:
        copy.wait()
    out_ref[...] = slots[...]


def slotted(stats, nv, ident):
    return pl.pallas_call(
        functools.partial(exchange_kernel, nv),
        out_shape=jax.ShapeDtypeStruct((nv,) + stats.shape, F32),
        in_specs=[pl.BlockSpec(memory_space=pltpu.VMEM)],
        out_specs=pl.BlockSpec(memory_space=pltpu.VMEM),
        scratch_shapes=[
            pltpu.VMEM((nv,) + stats.shape, F32),
            pltpu.SemaphoreType.DMA((nv - 1,)),
            pltpu.SemaphoreType.DMA((nv - 1,)),
        ],
        compiler_params=pltpu.CompilerParams(collective_id=ident, has_side_effects=True),
    )(stats)


def per_device(nt, nv, tok, teacher_hidden, teacher_head, student_hidden, student_head):
    head = teacher_head[0]
    columns = lax.all_to_all(student_hidden, "teacher", split_axis=1, concat_axis=0, tiled=True)
    partial_slog = jnp.dot(columns, student_head, preferred_element_type=F32)
    hidden, partial_slog = gather_hidden(teacher_hidden[0], nv, partial_slog)
    slog = lax.psum_scatter(partial_slog, "teacher", scatter_dimension=0, tiled=True)

    logits = jnp.dot(hidden, head, preferred_element_type=F32)
    m = jnp.max(logits, axis=-1)
    e = jnp.exp(logits - m[:, None])
    st = slotted(jnp.stack([m, jnp.sum(e, axis=-1), jnp.sum(e * logits, axis=-1)]), nv, 0)
    top = jnp.max(st[:, 0], axis=0)
    scale = jnp.exp(st[:, 0] - top)
    total = jnp.sum(st[:, 1] * scale, axis=0)
    moment = jnp.sum(st[:, 2] * scale, axis=0)
    lse = top + jnp.log(total)
    confid = jnp.exp(moment / total - lse)
    weighted = confid[:, None] * (logits - lse[:, None])
    slog, weighted = lax.optimization_barrier((slog, weighted))
    wsum = lax.psum_scatter(weighted, "teacher", scatter_dimension=0, tiled=True)
    csum = lax.psum_scatter(confid, "teacher", scatter_dimension=0, tiled=True)

    raw = wsum / csum[:, None]
    ms = jnp.max(slog, axis=-1)
    ss = jnp.sum(jnp.exp(slog - ms[:, None]), axis=-1)
    mr = jnp.max(raw, axis=-1)
    er = jnp.exp(raw - mr[:, None])
    st = slotted(
        jnp.stack([mr, jnp.sum(er, axis=-1), jnp.sum(er * (raw - slog), axis=-1), ms, ss]), nv, 1
    )
    tr = jnp.max(st[:, 0], axis=0)
    cr = jnp.exp(st[:, 0] - tr)
    total_r = jnp.sum(st[:, 1] * cr, axis=0)
    cross = jnp.sum(st[:, 2] * cr, axis=0)
    ts = jnp.max(st[:, 3], axis=0)
    total_s = jnp.sum(st[:, 4] * jnp.exp(st[:, 3] - ts), axis=0)
    lse_r = tr + jnp.log(total_r)
    lse_s = ts + jnp.log(total_s)
    kl = cross / total_r - lse_r + lse_s
    gradl = (jnp.exp(slog - lse_s[:, None]) - jnp.exp(raw - lse_r[:, None])).astype(jnp.bfloat16)
    all_grads = lax.all_gather(gradl, "teacher", axis=0, tiled=True)
    loss = lax.psum(jnp.sum(kl), "teacher") / tok
    all_grads, loss = lax.optimization_barrier((all_grads, loss))

    feats = student_head.shape[0]
    gh = lax.dot_general(
        all_grads, student_head, (((1,), (1,)), ((), ())), preferred_element_type=F32
    )
    gh = lax.psum_scatter(gh, "vocab", scatter_dimension=0, tiled=True)
    grad_weight = lax.dot_general(
        columns, all_grads, (((0,), (0,)), ((), ())), preferred_element_type=F32
    )
    gh, grad_weight = lax.optimization_barrier((gh, grad_weight))
    return loss, spread(nt, nv, gh, feats), grad_weight


def fused(nt, nv, tok, teacher_hidden, teacher_head, student_hidden, student_head):
    head, shead = teacher_head[0].T, student_head.T
    logits, stat, slog, columns = forward(teacher_hidden[0], head, student_hidden, shead, nv, 0)
    gradl, kl = combine(logits, stat, slog, nv, 1)
    loss = lax.psum(jnp.sum(kl[0]), "teacher") / tok
    every = lax.all_gather(gradl, "teacher", axis=1, tiled=True)
    gh = lax.dot_general(every, shead, (((0,), (0,)), ((), ())), preferred_element_type=F32)
    gh = lax.psum_scatter(gh, "vocab", scatter_dimension=0, tiled=True)
    grad_weight = lax.dot_general(every, columns, (((1,), (0,)), ((), ())), preferred_element_type=F32)
    gh, grad_weight = lax.optimization_barrier((gh, grad_weight))
    return loss, spread(nt, nv, gh, columns.shape[1]), grad_weight.T


def fits(nt, nv, tok, width):
    own = tok // nt
    return nt == 4 and nv == 2 * nt and own % 256 == 0 and width % (TURNS * META) == 0


def solution(mesh):
    nt, nv = mesh.shape["teacher"], mesh.shape["vocab"]

    def whole(teacher_hidden, teacher_head, student_hidden, student_head):
        tok = student_hidden.shape[0]
        step = fused if fits(nt, nv, tok, student_head.shape[1] // nv) else per_device
        return jax.shard_map(
            lambda *a: step(nt, nv, tok, *a),
            mesh=mesh,
            in_specs=(
                P("teacher", "vocab", None),
                P("teacher", None, "vocab"),
                P("teacher", None),
                P("teacher", "vocab"),
            ),
            out_specs=(P(), P("teacher", "vocab"), P("teacher", "vocab")),
            check_vma=False,
        )(teacher_hidden, teacher_head, student_hidden, student_head)

    return whole
```

```python
import functools

import jax
import jax.numpy as jnp
from jax import lax
from jax.experimental import pallas as pl
from jax.experimental.pallas import tpu as pltpu
from jax.sharding import PartitionSpec as P

F32 = jnp.float32
BF16 = jnp.bfloat16
MESH = pl.DeviceIdType.MESH
STEPS = 5
TURNS = 2 * STEPS
META = 16
OCT = 125.0
PIECES = 4
SLOTS = 5
AHEAD = 5


def fold(x, op):
    return op(x.reshape(x.shape[0] // 8, 8, x.shape[1]), axis=0)


def level(top):
    return (top * 1.01 + 1e-30).astype(BF16).astype(F32)


def push(src, dst, ssem, rsem, **to):
    return pltpu.make_async_remote_copy(
        src_ref=src, dst_ref=dst, send_sem=ssem, recv_sem=rsem, device_id=to, device_id_type=MESH
    )


def square():
    t = lax.axis_index("teacher")
    return t, t + 1 - 2 * lax.rem(t, 2), lax.rem(t + 2, 4), 3 - t


def sub_rows(rows):
    for n in (80, 64, 48, 32, 16):
        if rows % n == 0:
            return n


class Halving:
    def __init__(self, bufs, part):
        self.s1, self.r1, self.s2, self.r2, self.ss1, self.sr1, self.ss2, self.sr2 = bufs
        self.part = part
        self.sub = sub_rows(part)
        self.t, self.px, self.py, self.across = square()

    def near(self, i):
        return jnp.where(lax.rem(i, 2) == 0, self.px, self.py)

    def far(self, i):
        return jnp.where(lax.rem(i, 2) == 0, self.py, self.px)

    def first(self, i):
        return push(self.s1.at[i], self.r1.at[i], self.ss1.at[i], self.sr1.at[i], teacher=self.near(i))

    def second(self, i):
        return push(self.s2.at[i], self.r2.at[i], self.ss2.at[i], self.sr2.at[i], teacher=self.far(i))

    def meta(self, reach, c):
        hi = c.astype(BF16).astype(F32)
        mid = (c - hi).astype(BF16).astype(F32)
        lo = c - hi - mid
        row = lax.broadcasted_iota(jnp.int32, (META, c.shape[1]), 0)
        rows = jnp.where(row == 0, reach, jnp.where(row == 1, hi, jnp.where(row == 2, mid, lo)))
        return rows.astype(BF16)

    def read_meta(self, ref):
        m = ref[pl.ds(self.part, META), :].astype(F32)
        return m[0:1], m[1:2] + m[2:3] + m[3:4]

    def loop(self, body):
        def one(j, carry):
            body(pl.ds(pl.multiple_of(j * self.sub, self.sub), self.sub))
            return carry

        lax.fori_loop(0, self.part // self.sub, one, 0)

    def send(self, i, value, top, weight):
        for b, owner in enumerate((self.near(i), self.across)):
            reach = level(top(i, owner))
            rate = OCT / reach
            dst = self.s1.at[i, b]

            def body(rows):
                dst[rows, :] = jnp.exp2(value(i, owner, rows) * rate).astype(BF16)

            self.loop(body)
            dst[pl.ds(self.part, META), :] = self.meta(reach, weight(owner))
        self.first(i).start()

    def relay(self, i, value, top, weight):
        self.first(i).wait_recv()
        owner = self.far(i)
        src = self.r1.at[i, 1]
        dst = self.s2.at[i]
        r, c = self.read_meta(src)
        reach = level(r + top(i, owner))
        rate = OCT / reach
        back = r * (1.0 / OCT)

        def body(rows):
            y = jnp.log2(src[rows, :].astype(F32)) * back
            dst[rows, :] = jnp.exp2((value(i, owner, rows) + y) * rate).astype(BF16)

        self.loop(body)
        dst[pl.ds(self.part, META), :] = self.meta(reach, c + weight(owner))
        self.second(i).start()

    def finish(self, i, value, weight, emit):
        self.second(i).wait_recv()
        one, two = self.r1.at[i, 0], self.r2.at[i]
        r1, c1 = self.read_meta(one)
        r2, c2 = self.read_meta(two)
        k1, k2 = r1 * (1.0 / OCT), r2 * (1.0 / OCT)
        total = c1 + c2 + weight(self.t)

        def body(rows):
            y = jnp.log2(one[rows, :].astype(F32)) * k1
            z = jnp.log2(two[rows, :].astype(F32)) * k2
            emit(i, rows, value(i, self.t, rows) + y + z, total)

        self.loop(body)

    def drain(self):
        def one(i, carry):
            self.first(i).wait_send()
            self.second(i).wait_send()
            return carry

        lax.fori_loop(0, TURNS, one, 0)


def halving_scratch(part, own):
    sem = pltpu.SemaphoreType.DMA((TURNS,))
    one, two = (TURNS, 2, part + META, own), (TURNS, part + META, own)
    return [pltpu.VMEM(one, BF16)] * 2 + [pltpu.VMEM(two, BF16)] * 2 + [sem] * 4


def turn_row(i, width, part):
    return lax.rem(i, 2) * (width // 2) + i // 2 * part


NT = (((1,), (1,)), ((), ()))


def forward_kernel(chips, th, head, sh, shead, logits, stat, slog, cols, *scratch):
    halving = Halving(scratch[:8], head.shape[0] // TURNS)
    (hid, wbuf, ws, work, tops, ends, acc, wsem, vsem, lsem, outsem, zs, zr, cs, cr, os_, or_, fs, fr, gs, gr) = scratch[8:]
    width = head.shape[0]
    part = width // TURNS
    rows = th.shape[0]
    piece = rows // PIECES
    feats = ws.shape[2]
    own = sh.shape[0]
    hops = chips - 1
    tiles = TURNS
    t = halving.t
    v = lax.axis_index("vocab")
    core = lax.rem(v, 2)
    chip = v // 2
    twin = v + 1 - 2 * core
    others = (halving.px, halving.py, halving.across)

    barrier = pltpu.get_barrier_semaphore()
    for p in others:
        pl.semaphore_signal(barrier, inc=1, device_id={"teacher": p}, device_id_type=MESH)
    pl.semaphore_signal(barrier, inc=1, device_id={"vocab": twin}, device_id_type=MESH)

    @pl.when(chip > 0)
    def _():
        pl.semaphore_signal(barrier, inc=1, device_id={"vocab": v - 2}, device_id_type=MESH)

    @pl.when(chip < chips - 1)
    def _():
        pl.semaphore_signal(barrier, inc=1, device_id={"vocab": v + 2}, device_id_type=MESH)

    def tile_copy(g):
        slot = lax.rem(g, AHEAD)
        at = pl.ds(pl.multiple_of(lax.rem(g, tiles) * part, part), part)
        return pltpu.make_async_copy(head.at[at], wbuf.at[slot], wsem.at[slot])

    def lanes(n):
        return pl.ds(pl.multiple_of(n * feats, feats), feats)

    def block(s, c):
        return pl.ds(pl.multiple_of((s * 2 + c) * rows, rows), rows)

    own_hid = pltpu.make_async_copy(th, hid.at[block(chip, core)], lsem.at[0])
    own_cols = pltpu.make_async_copy(sh.at[:, lanes(t)], cols.at[pl.ds(pl.multiple_of(t * own, own), own)], lsem.at[1])

    def ws_copy(i):
        at = pl.ds(pl.multiple_of(turn_row(i, width, part), META), part)
        return pltpu.make_async_copy(shead.at[at], ws.at[lax.rem(i, 2)], vsem.at[lax.rem(i, 2)])

    own_hid.start()
    for g in range(AHEAD - 1):
        tile_copy(g).start()
    own_cols.start()
    ws_copy(0).start()

    @pl.when((chip > 0) & (chip < chips - 1))
    def _():
        pl.semaphore_wait(barrier, 6)

    @pl.when((chip == 0) | (chip == chips - 1))
    def _():
        pl.semaphore_wait(barrier, 5)

    half = own // 2

    def col_rows(owner):
        return pl.ds(pl.multiple_of(owner * own + core * half, half), half)

    def col_out(n):
        src = sh.at[pl.ds(pl.multiple_of(core * half, half), half), lanes(others[n])]
        return push(src, cols.at[col_rows(t)], fs.at[n], fr.at[n], teacher=others[n])

    def col_twin(n):
        at = cols.at[col_rows(others[n])]
        return push(at, at, gs.at[n], gr.at[n], vocab=twin)

    for n in range(3):
        col_out(n).start()

    twin_own = push(th, hid.at[block(chip, core)], os_.at[0], or_.at[0], vocab=twin)
    twin_own.start()

    def at(s, q):
        return hid.at[pl.ds(pl.multiple_of((s * 2 + core) * rows + q * piece, piece), piece)]

    def along(d, h, q):
        s = chip - h if d == 0 else chip + h
        return push(at(s, q), at(s, q), zs.at[d, h, q], zr.at[d, h, q], vocab=v + 2 if d == 0 else v - 2)

    def arrived(d, h, q):
        s = chip - 1 - h if d == 0 else chip + 1 + h
        return push(at(s, q), at(s, q), zs.at[d, h, q], zr.at[d, h, q], vocab=v + 2 if d == 0 else v - 2)

    def across(d, h, q):
        s = chip - 1 - h if d == 0 else chip + 1 + h
        return push(at(s, q), at(s, q), cs.at[d, h, q], cr.at[d, h, q], vocab=twin)

    def arrives(d, h):
        return chip - 1 - h >= 0 if d == 0 else chip + 1 + h <= chips - 1

    def sends(d, h):
        return (chip - h >= 0) & (chip + 1 <= chips - 1) if d == 0 else (chip + h <= chips - 1) & (chip >= 1)

    own_hid.wait()
    for d in range(2):

        @pl.when(sends(d, 0))
        def _():
            for q in range(PIECES):
                along(d, 0, q).start()

    def event(j, carry):
        h = j // PIECES
        q = lax.rem(j, PIECES)
        for d in range(2):

            @pl.when(arrives(d, h))
            def _():
                arrived(d, h, q).wait_recv()
                across(d, h, q).start()

            @pl.when(arrives(d, h) & sends(d, h + 1))
            def _():
                along(d, h + 1, q).start()

        return carry

    short = jnp.minimum(chip, chips - 1 - chip)

    def source(p):
        d = (p + 1) // 2
        near = jnp.where(lax.rem(p, 2) == 1, chip - d, chip + d)
        beyond = jnp.where(chip == short, chip + p - short, chip - p + short)
        return jnp.where(p <= 2 * short, near, beyond)

    def flush(s):
        return pltpu.make_async_copy(acc, logits.at[s], outsem.at[0])

    def tile(g, carry):
        p = g // tiles
        kt = lax.rem(g, tiles)
        s = source(p)

        @pl.when(g + AHEAD - 1 < chips * tiles)
        def _():
            tile_copy(g + AHEAD - 1).start()

        @pl.when(kt == 0)
        def _():
            @pl.when(p == 0)
            def _():
                twin_own.wait_recv()

            for d in range(2):

                @pl.when((s < chip) if d == 0 else (s > chip))
                def _():
                    h = (chip - s if d == 0 else s - chip) - 1
                    for q in range(PIECES):
                        across(d, h, q).wait_recv()

            @pl.when(p > 0)
            def _():
                flush(0).wait()

            big = jnp.full((8, 2 * rows), 3e38, F32)
            ends[0] = -big
            ends[1] = big

        tile_copy(g).wait()
        a = hid[pl.ds(pl.multiple_of(s * 2 * rows, 2 * rows), 2 * rows), :]
        x = lax.dot_general(wbuf[lax.rem(g, AHEAD)], a, NT, preferred_element_type=F32)
        acc[pl.ds(pl.multiple_of(kt * part, part), part), :] = x
        ends[0] = jnp.maximum(ends[0], fold(x, jnp.max))
        ends[1] = jnp.minimum(ends[1], fold(x, jnp.min))

        @pl.when(kt == tiles - 1)
        def _():
            flush(s).start()
            sub = halving.sub
            n = 2 * rows

            m = jnp.max(ends[0], axis=0, keepdims=True)

            def sums(j, c):
                x = acc[pl.ds(pl.multiple_of(j * sub, sub), sub), :]
                e = jnp.exp(x - m)
                return c[0] + fold(e, jnp.sum), c[1] + fold(e * x, jnp.sum)

            zero = jnp.zeros((8, n), F32)
            z, f = lax.fori_loop(0, width // sub, sums, (zero, zero))
            z, f = jnp.sum(z, axis=0, keepdims=True), jnp.sum(f, axis=0, keepdims=True)
            low = jnp.min(ends[1], axis=0, keepdims=True)
            row = lax.broadcasted_iota(jnp.int32, (8, n), 0)
            stat[s] = jnp.where(row == 0, m, jnp.where(row == 1, z, jnp.where(row == 2, f, low)))

        return carry

    lax.fori_loop(0, tiles - 2, tile, 0)
    for n in range(3):
        col_out(n).wait_recv()
        col_twin(n).start()
    lax.fori_loop(tiles - 2, tiles, tile, 0)
    for n in range(3):
        col_twin(n).wait_recv()
    own_cols.wait()

    def value(i, owner, r):
        return work[lax.rem(i, SLOTS), owner, r, :]

    def top(i, owner):
        return jnp.max(tops[lax.rem(i, SLOTS), owner], axis=0, keepdims=True)

    def weight(owner):
        return jnp.ones((1, own), F32)

    def emit(i, r, x, c):
        slog[pl.ds(pl.multiple_of(turn_row(i, width, part) + r.start, halving.sub), halving.sub), :] = x

    events = hops * PIECES

    def seen(i):
        return jnp.where(i < 0, 0, jnp.minimum(2 + 6 * jnp.maximum(i, 0) // 5, events))

    def done(i):
        one = jnp.minimum(tiles + 4 * jnp.maximum(i - 1, 0), 2 * tiles)
        two = jnp.minimum(2 * tiles + 3 * jnp.maximum(i - 4, 0), 3 * tiles)
        three = jnp.minimum(3 * tiles + 4 * jnp.maximum(i - 8, 0), 4 * tiles)
        return jnp.where(i < 5, one, jnp.where(i < 9, two, three))

    def turn(i, carry):
        lax.fori_loop(seen(i - 1), seen(i), event, 0)

        @pl.when(i < TURNS)
        def _():
            @pl.when(i + 1 < TURNS)
            def _():
                ws_copy(i + 1).start()

            ws_copy(i).wait()
            a = ws[lax.rem(i, 2)]
            for owner in range(4):
                x = lax.dot_general(a, cols[pl.ds(owner * own, own), :], NT, preferred_element_type=F32)
                work[lax.rem(i, SLOTS), owner] = x
                tops[lax.rem(i, SLOTS), owner] = fold(jnp.abs(x), jnp.max)
            halving.send(i, value, top, weight)

        @pl.when((i >= 2) & (i < TURNS + 2))
        def _():
            halving.relay(i - 2, value, top, weight)

        @pl.when(i >= 4)
        def _():
            halving.finish(i - 4, value, weight, emit)

        lax.fori_loop(done(i - 1), done(i), tile, 0)
        return carry

    lax.fori_loop(0, TURNS + 4, turn, 0)

    flush(0).wait()
    halving.drain()
    for n in range(3):
        col_out(n).wait_send()
        col_twin(n).wait_send()
    twin_own.wait_send()

    def sent(j, carry):
        h = j // PIECES
        q = lax.rem(j, PIECES)
        for d in range(2):

            @pl.when(sends(d, h))
            def _():
                along(d, h, q).wait_send()

            @pl.when(arrives(d, h))
            def _():
                across(d, h, q).wait_send()

        return carry

    lax.fori_loop(0, events, sent, 0)


def forward(th, head, sh, shead, nv, ident):
    chips = nv // 2
    rows, depth = th.shape
    width = head.shape[0]
    feats = shead.shape[1]
    own = sh.shape[0]
    part = width // TURNS
    hops = chips - 1
    hbm = pl.BlockSpec(memory_space=pl.ANY)
    vmem = pl.BlockSpec(memory_space=pltpu.VMEM)
    dma = pltpu.SemaphoreType.DMA
    relays = dma((2, hops, PIECES))
    return pl.pallas_call(
        functools.partial(forward_kernel, chips),
        out_shape=(
            jax.ShapeDtypeStruct((chips, width, 2 * rows), F32),
            jax.ShapeDtypeStruct((chips, 8, 2 * rows), F32),
            jax.ShapeDtypeStruct((width, own), F32),
            jax.ShapeDtypeStruct((4 * own, feats), BF16),
        ),
        in_specs=[hbm] * 4,
        out_specs=(hbm, vmem, vmem, vmem),
        scratch_shapes=halving_scratch(part, own)
        + [
            pltpu.VMEM((nv * rows, depth), BF16),
            pltpu.VMEM((AHEAD, part, depth), BF16),
            pltpu.VMEM((2, part, feats), BF16),
            pltpu.VMEM((SLOTS, 4, part, own), F32),
            pltpu.VMEM((SLOTS, 4, 8, own), F32),
            pltpu.VMEM((2, 8, 2 * rows), F32),
            pltpu.VMEM((width, 2 * rows), F32),
            dma((AHEAD,)),
            dma((2,)),
            dma((2,)),
            dma((1,)),
            relays,
            relays,
            relays,
            relays,
            dma((1,)),
            dma((1,)),
            dma((3,)),
            dma((3,)),
            dma((3,)),
            dma((3,)),
        ],
        compiler_params=pltpu.CompilerParams(
            collective_id=ident, has_side_effects=True, vmem_limit_bytes=60 * 2**20
        ),
        name="forward",
    )(th, head, sh, shead)


def combine_kernel(nv, logits, stat, slog, grad, kl, *scratch):
    width, own = slog.shape
    part = width // TURNS
    halving = Halving(scratch[:8], part)
    lg, raw, peak, st, mine, st2, lsem, ssem, rsem, ssem2, rsem2 = scratch[8:]
    t = halving.t
    v = lax.axis_index("vocab")
    sub = halving.sub

    def fetch(n, owner):
        return pltpu.make_async_copy(logits.at[owner], lg.at[owner], lsem.at[n])

    order = (halving.px, halving.across, halving.py, t)
    for n in range(4):
        fetch(n, order[n]).start()

    barrier = pltpu.get_barrier_semaphore()
    for p in (halving.px, halving.py):
        pl.semaphore_signal(barrier, inc=1, device_id={"teacher": p}, device_id_type=MESH)
    for n in range(1, nv):
        pl.semaphore_signal(barrier, inc=1, device_id={"vocab": lax.rem(v + n, nv)}, device_id_type=MESH)
    pl.semaphore_wait(barrier, nv + 1)

    def share(n, src, dst, ss, rs):
        return push(src, dst.at[v], ss.at[n - 1], rs.at[n - 1], vocab=lax.rem(v + n, nv))

    for n in range(1, nv):
        share(n, stat, st, ssem, rsem).start()
    st[v] = stat[...]

    zero = jnp.zeros((8, own), F32)

    def at(j):
        return pl.ds(pl.multiple_of(j * sub, sub), sub)

    def student():
        m = lax.fori_loop(0, width // sub, lambda j, c: jnp.maximum(c, fold(slog[at(j), :], jnp.max)), zero - 3e38)
        m = jnp.max(m, axis=0, keepdims=True)
        z = lax.fori_loop(0, width // sub, lambda j, c: c + fold(jnp.exp(slog[at(j), :] - m), jnp.sum), zero)
        peak[1] = jnp.broadcast_to(m, (8, own))
        peak[2] = z

    for n in range(1, nv):
        share(n, stat, st, ssem, rsem).wait()

    for o in range(4):
        m = [st[s, o, 0:1, :] for s in range(nv)]
        big = functools.reduce(jnp.maximum, m)
        scale = [jnp.exp(x - big) for x in m]
        total = sum(st[s, o, 1:2, :] * scale[s] for s in range(nv))
        moment = sum(st[s, o, 2:3, :] * scale[s] for s in range(nv))
        lse = big + jnp.log(total)
        conf = jnp.exp(moment / total - lse)
        reach = conf * jnp.maximum(jnp.abs(stat[o, 0:1, :] - lse), jnp.abs(stat[o, 3:4, :] - lse))
        row = lax.broadcasted_iota(jnp.int32, (8, own), 0)
        mine[o] = jnp.where(row == 0, conf, jnp.where(row == 1, lse, reach))
    for n in range(2):
        fetch(n, order[n]).wait()

    def value(i, owner, r):
        rows = pl.ds(pl.multiple_of(turn_row(i, width, part) + r.start, sub), sub)
        return mine[owner, 0:1, :] * (lg[owner, rows, :] - mine[owner, 1:2, :])

    def top(i, owner):
        return mine[owner, 2:3, :]

    def weight(owner):
        return mine[owner, 0:1, :]

    peak[0] = zero - 3e38

    def emit(i, r, x, c):
        rows = pl.ds(pl.multiple_of(turn_row(i, width, part) + r.start, sub), sub)
        x = x * (1.0 / c)
        raw[rows, :] = x
        peak[0] = jnp.maximum(peak[0], fold(x, jnp.max))

    def turn(i, carry):
        for n in (2, 3):

            @pl.when(i == n - 1)
            def _():
                fetch(n, order[n]).wait()

        @pl.when(i < TURNS)
        def _():
            halving.send(i, value, top, weight)

        @pl.when(i == 1)
        def _():
            student()

        @pl.when((i >= 2) & (i < TURNS + 2))
        def _():
            halving.relay(i - 2, value, top, weight)

        @pl.when(i >= 4)
        def _():
            halving.finish(i - 4, value, weight, emit)

        return carry

    lax.fori_loop(0, TURNS + 4, turn, 0)

    mr = jnp.max(peak[0], axis=0, keepdims=True)
    ms = peak[1, 0:1]
    ss = jnp.sum(peak[2], axis=0, keepdims=True)

    def sums(j, c):
        x = raw[at(j), :]
        e = jnp.exp(x - mr)
        return c[0] + fold(e, jnp.sum), c[1] + fold(e * (x - slog[at(j), :]), jnp.sum)

    sr, cross = lax.fori_loop(0, width // sub, sums, (zero, zero))
    sr, cross = jnp.sum(sr, axis=0, keepdims=True), jnp.sum(cross, axis=0, keepdims=True)
    row = lax.broadcasted_iota(jnp.int32, (8, own), 0)
    mine[0] = jnp.where(
        row == 0, mr, jnp.where(row == 1, sr, jnp.where(row == 2, cross, jnp.where(row == 3, ms, ss)))
    )
    for n in range(1, nv):
        share(n, mine.at[0], st2, ssem2, rsem2).start()
    st2[v] = mine[0]
    halving.drain()
    for n in range(1, nv):
        share(n, mine.at[0], st2, ssem2, rsem2).wait()
    every = [st2[s] for s in range(nv)]
    tr = functools.reduce(jnp.maximum, [x[0:1] for x in every])
    ts = functools.reduce(jnp.maximum, [x[3:4] for x in every])
    cr = [jnp.exp(x[0:1] - tr) for x in every]
    total_r = sum(x[1:2] * c for x, c in zip(every, cr))
    cross = sum(x[2:3] * c for x, c in zip(every, cr))
    total_s = sum(x[4:5] * jnp.exp(x[3:4] - ts) for x in every)
    lse_r = tr + jnp.log(total_r)
    lse_s = ts + jnp.log(total_s)
    kl[...] = jnp.broadcast_to(cross / total_r - lse_r + lse_s, (8, own))

    def grads(j, c):
        grad[at(j), :] = (jnp.exp(slog[at(j), :] - lse_s) - jnp.exp(raw[at(j), :] - lse_r)).astype(BF16)
        return c

    lax.fori_loop(0, width // sub, grads, 0)


def combine(logits, stat, slog, nv, ident):
    width, own = slog.shape
    part = width // TURNS
    hbm = pl.BlockSpec(memory_space=pl.ANY)
    vmem = pl.BlockSpec(memory_space=pltpu.VMEM)
    dma = pltpu.SemaphoreType.DMA
    return pl.pallas_call(
        functools.partial(combine_kernel, nv),
        out_shape=(jax.ShapeDtypeStruct((width, own), BF16), jax.ShapeDtypeStruct((8, own), F32)),
        in_specs=[hbm, vmem, vmem],
        out_specs=(vmem, vmem),
        scratch_shapes=halving_scratch(part, own)
        + [
            pltpu.VMEM((4, width, own), F32),
            pltpu.VMEM((width, own), F32),
            pltpu.VMEM((3, 8, own), F32),
            pltpu.VMEM((nv, 4, 8, own), F32),
            pltpu.VMEM((4, 8, own), F32),
            pltpu.VMEM((nv, 8, own), F32),
            dma((4,)),
            dma((nv - 1,)),
            dma((nv - 1,)),
            dma((nv - 1,)),
            dma((nv - 1,)),
        ],
        compiler_params=pltpu.CompilerParams(
            collective_id=ident, has_side_effects=True, vmem_limit_bytes=60 * 2**20
        ),
        name="combine",
    )(logits, stat, slog)


def spread(nt, nv, gh, feats):
    r = nv // nt
    part = lax.rem(lax.axis_index("vocab"), r)
    rows, width = gh.shape[0], feats // r
    grad_hidden = jnp.zeros((r, rows, width), F32)
    for k in range(r):
        swap = [
            (s * nv + t * r + h, t * nv + s * r + (h + k) % r)
            for s in range(nt)
            for t in range(nt)
            for h in range(r)
        ]
        piece = lax.dynamic_slice(gh, (0, lax.rem(part + k, r) * width), (rows, width))
        piece = lax.ppermute(piece, ("teacher", "vocab"), swap)
        grad_hidden = lax.dynamic_update_slice(
            grad_hidden, piece[None], (lax.rem(part + r - k, r), 0, 0)
        )
    return grad_hidden.reshape(r * rows, width)


def gather_hidden(own, nv, first):
    chips = nv // 2
    at = lax.axis_index("vocab")
    chip = at // 2
    up = [own]
    down = [own]
    for hop in range(chips - 1):
        up.append(lax.ppermute(up[-1], "vocab", [(i, i + 2) for i in range(nv - 2)]))
        down.append(lax.ppermute(down[-1], "vocab", [(i + 2, i) for i in range(nv - 2)]))
        if hop == 1:
            up[-1], down[-1], first = lax.optimization_barrier((up[-1], down[-1], first))
    pair = [(i, i ^ 1) for i in range(nv)]
    rows, width = own.shape
    buf = jnp.zeros((chips, 2, rows, width), own.dtype)
    core = at % 2
    for k in range(chips):
        piece = own if k == 0 else up[k] + down[chips - k]
        other = lax.ppermute(piece, "vocab", pair)
        slot = lax.rem(chip - k + chips, chips)
        buf = lax.dynamic_update_slice(buf, piece[None, None], (slot, core, 0, 0))
        buf = lax.dynamic_update_slice(buf, other[None, None], (slot, 1 - core, 0, 0))
    return buf.reshape(nv * rows, width), first


def exchange_kernel(nv, own_ref, out_ref, slots, send, recv):
    me = lax.axis_index("vocab")
    barrier = pltpu.get_barrier_semaphore()
    for step in range(1, nv):
        pl.semaphore_signal(
            barrier,
            inc=1,
            device_id={"vocab": lax.rem(me + step, nv)},
            device_id_type=pl.DeviceIdType.MESH,
        )
    pl.semaphore_wait(barrier, nv - 1)
    copies = []
    for step in range(1, nv):
        copies.append(
            pltpu.make_async_remote_copy(
                src_ref=own_ref,
                dst_ref=slots.at[me],
                send_sem=send.at[step - 1],
                recv_sem=recv.at[step - 1],
                device_id={"vocab": lax.rem(me + step, nv)},
                device_id_type=pl.DeviceIdType.MESH,
            )
        )
        copies[-1].start()
    slots[me] = own_ref[...]
    for copy in copies:
        copy.wait()
    out_ref[...] = slots[...]


def slotted(stats, nv, ident):
    return pl.pallas_call(
        functools.partial(exchange_kernel, nv),
        out_shape=jax.ShapeDtypeStruct((nv,) + stats.shape, F32),
        in_specs=[pl.BlockSpec(memory_space=pltpu.VMEM)],
        out_specs=pl.BlockSpec(memory_space=pltpu.VMEM),
        scratch_shapes=[
            pltpu.VMEM((nv,) + stats.shape, F32),
            pltpu.SemaphoreType.DMA((nv - 1,)),
            pltpu.SemaphoreType.DMA((nv - 1,)),
        ],
        compiler_params=pltpu.CompilerParams(collective_id=ident, has_side_effects=True),
    )(stats)


def per_device(nt, nv, tok, teacher_hidden, teacher_head, student_hidden, student_head):
    head = teacher_head[0]
    columns = lax.all_to_all(student_hidden, "teacher", split_axis=1, concat_axis=0, tiled=True)
    partial_slog = jnp.dot(columns, student_head, preferred_element_type=F32)
    hidden, partial_slog = gather_hidden(teacher_hidden[0], nv, partial_slog)
    slog = lax.psum_scatter(partial_slog, "teacher", scatter_dimension=0, tiled=True)

    logits = jnp.dot(hidden, head, preferred_element_type=F32)
    m = jnp.max(logits, axis=-1)
    e = jnp.exp(logits - m[:, None])
    st = slotted(jnp.stack([m, jnp.sum(e, axis=-1), jnp.sum(e * logits, axis=-1)]), nv, 0)
    top = jnp.max(st[:, 0], axis=0)
    scale = jnp.exp(st[:, 0] - top)
    total = jnp.sum(st[:, 1] * scale, axis=0)
    moment = jnp.sum(st[:, 2] * scale, axis=0)
    lse = top + jnp.log(total)
    confid = jnp.exp(moment / total - lse)
    weighted = confid[:, None] * (logits - lse[:, None])
    slog, weighted = lax.optimization_barrier((slog, weighted))
    wsum = lax.psum_scatter(weighted, "teacher", scatter_dimension=0, tiled=True)
    csum = lax.psum_scatter(confid, "teacher", scatter_dimension=0, tiled=True)

    raw = wsum / csum[:, None]
    ms = jnp.max(slog, axis=-1)
    ss = jnp.sum(jnp.exp(slog - ms[:, None]), axis=-1)
    mr = jnp.max(raw, axis=-1)
    er = jnp.exp(raw - mr[:, None])
    st = slotted(
        jnp.stack([mr, jnp.sum(er, axis=-1), jnp.sum(er * (raw - slog), axis=-1), ms, ss]), nv, 1
    )
    tr = jnp.max(st[:, 0], axis=0)
    cr = jnp.exp(st[:, 0] - tr)
    total_r = jnp.sum(st[:, 1] * cr, axis=0)
    cross = jnp.sum(st[:, 2] * cr, axis=0)
    ts = jnp.max(st[:, 3], axis=0)
    total_s = jnp.sum(st[:, 4] * jnp.exp(st[:, 3] - ts), axis=0)
    lse_r = tr + jnp.log(total_r)
    lse_s = ts + jnp.log(total_s)
    kl = cross / total_r - lse_r + lse_s
    gradl = (jnp.exp(slog - lse_s[:, None]) - jnp.exp(raw - lse_r[:, None])).astype(jnp.bfloat16)
    all_grads = lax.all_gather(gradl, "teacher", axis=0, tiled=True)
    loss = lax.psum(jnp.sum(kl), "teacher") / tok
    all_grads, loss = lax.optimization_barrier((all_grads, loss))

    feats = student_head.shape[0]
    gh = lax.dot_general(
        all_grads, student_head, (((1,), (1,)), ((), ())), preferred_element_type=F32
    )
    gh = lax.psum_scatter(gh, "vocab", scatter_dimension=0, tiled=True)
    grad_weight = lax.dot_general(
        columns, all_grads, (((0,), (0,)), ((), ())), preferred_element_type=F32
    )
    gh, grad_weight = lax.optimization_barrier((gh, grad_weight))
    return loss, spread(nt, nv, gh, feats), grad_weight


def gather_kernel(nv, grad, kl, shead, every, mine, away, loss, *scratch):
    g, ws, gh, rx, sums, a_s, a_r, b_s, b_r, c_s, c_r, x_s, x_r, l_s, l_r, lsem, fsem = scratch
    width, own = grad.shape
    feats = ws.shape[1]
    part = width // TURNS
    rows = 4 * own // nv
    chips = nv // 2
    t, px, py, diagonal = square()
    v = lax.axis_index("vocab")
    core = lax.rem(v, 2)
    chip = v // 2
    twin = v + 1 - 2 * core
    own_ws = pltpu.make_async_copy(shead, ws, lsem.at[0])
    own_ws.start()

    def span(i):
        return pl.ds(pl.multiple_of(turn_row(i, width, part), META), part)

    def lanes(owner):
        return pl.ds(pl.multiple_of(owner * own, own), own)

    own_g = pltpu.make_async_copy(grad, g.at[:, lanes(t)], lsem.at[1])
    own_g.start()
    barrier = pltpu.get_barrier_semaphore()
    for p in (px, py, diagonal):
        pl.semaphore_signal(barrier, inc=1, device_id={"teacher": p}, device_id_type=MESH)
    pl.semaphore_signal(barrier, inc=1, device_id={"vocab": twin}, device_id_type=MESH)
    pl.semaphore_wait(barrier, 4)

    def near(i):
        return jnp.where(lax.rem(i, 2) == 0, px, py)

    def far(i):
        return jnp.where(lax.rem(i, 2) == 0, py, px)

    def to_near(i):
        return push(grad.at[span(i)], g.at[span(i), lanes(t)], a_s.at[i], a_r.at[i], teacher=near(i))

    def to_far(i):
        return push(grad.at[span(i)], g.at[span(i), lanes(t)], b_s.at[i], b_r.at[i], teacher=far(i))

    def onward(i):
        at = g.at[span(i), lanes(near(i))]
        return push(at, at, c_s.at[i], c_r.at[i], teacher=far(i))

    def keep(i):
        return pltpu.make_async_copy(g.at[span(i)], every.at[span(i)], fsem.at[i])

    to_near(0).start()
    to_far(0).start()

    x = kl[...]
    lane = 128
    part_sum = sum(x[:, n * lane : (n + 1) * lane] for n in range(own // lane))
    sums[t] = part_sum
    others = (px, py, diagonal)

    def tell(n):
        return push(sums.at[t], sums.at[t], l_s.at[n], l_r.at[n], teacher=others[n])

    for n in range(3):
        tell(n).start()
    gh[...] = jnp.zeros_like(gh)
    own_ws.wait()
    own_g.wait()

    def turn(i, carry):
        @pl.when(i + 1 < TURNS)
        def _():
            to_near(i + 1).start()
            to_far(i + 1).start()

        @pl.when(i < TURNS)
        def _():
            to_near(i).wait_recv()
            onward(i).start()

        @pl.when(i >= 2)
        def _():
            k = i - 2
            to_far(k).wait_recv()
            onward(k).wait_recv()
            keep(k).start()
            b = ws[span(k), :]
            for owner in range(4):
                gh[pl.ds(owner * own, own), :] += lax.dot_general(
                    g[span(k), pl.ds(owner * own, own)], b, (((0,), (0,)), ((), ())), preferred_element_type=F32
                )

        return carry

    lax.fori_loop(0, TURNS + 2, turn, 0)

    def swap(c):
        src = gh.at[pl.ds(pl.multiple_of((2 * c + 1 - core) * rows, rows), rows)]
        return push(src, rx.at[c], x_s.at[c], x_r.at[c], vocab=twin)

    for c in range(chips):
        swap(c).start()
    for n in range(3):
        tell(n).wait()
    loss[...] = sums[0] + sums[1] + sums[2] + sums[3]
    for c in range(chips):
        swap(c).wait_recv()
        for f in range(feats // own):
            cut = pl.ds(f * own, own)
            x = gh[pl.ds(pl.multiple_of((2 * c + core) * rows, rows), rows), cut] + rx[c, :, cut]
            reach = level(jnp.max(fold(jnp.abs(x), jnp.max), axis=0, keepdims=True))
            away[c, pl.ds(0, rows), cut] = jnp.exp2(x * (OCT / reach)).astype(BF16)
            away[c, pl.ds(rows, META), cut] = jnp.broadcast_to(reach, (META, own)).astype(BF16)

            @pl.when(chip == c)
            def _():
                mine[:, cut] = x

    for c in range(chips):
        swap(c).wait_send()

    def drain(i, carry):
        to_near(i).wait_send()
        to_far(i).wait_send()
        onward(i).wait_send()
        keep(i).wait()
        return carry

    lax.fori_loop(0, TURNS, drain, 0)


def gather(grad, kl, shead, nv, ident):
    width, own = grad.shape
    feats = shead.shape[1]
    chips = nv // 2
    rows = 4 * own // nv
    hbm = pl.BlockSpec(memory_space=pl.ANY)
    vmem = pl.BlockSpec(memory_space=pltpu.VMEM)
    dma = pltpu.SemaphoreType.DMA
    return pl.pallas_call(
        functools.partial(gather_kernel, nv),
        out_shape=(
            jax.ShapeDtypeStruct((width, 4 * own), BF16),
            jax.ShapeDtypeStruct((rows, feats), F32),
            jax.ShapeDtypeStruct((chips, rows + META, feats), BF16),
            jax.ShapeDtypeStruct((8, 128), F32),
        ),
        in_specs=[vmem, vmem, hbm],
        out_specs=(hbm, vmem, vmem, vmem),
        scratch_shapes=[
            pltpu.VMEM((width, 4 * own), BF16),
            pltpu.VMEM((width, feats), BF16),
            pltpu.VMEM((4 * own, feats), F32),
            pltpu.VMEM((chips, rows, feats), F32),
            pltpu.VMEM((4, 8, 128), F32),
        ]
        + [dma((TURNS,))] * 6
        + [dma((chips,))] * 2
        + [dma((3,))] * 2
        + [dma((2,)), dma((TURNS,))],
        compiler_params=pltpu.CompilerParams(
            collective_id=ident, has_side_effects=True, vmem_limit_bytes=56 * 2**20
        ),
        name="gather",
    )(grad, kl, shead)


def spread_coded(nt, nv, gh, feats):
    r = nv // nt
    part = lax.rem(lax.axis_index("vocab"), r)
    rows, width = gh.shape[0], feats // r
    reach = lax.reduce_precision(jnp.max(jnp.abs(gh), axis=0, keepdims=True) * 1.01 + 1e-30, 8, 7)
    coded = jnp.concatenate([jnp.exp2(gh * (OCT / reach)), jnp.broadcast_to(reach, (META, feats))], axis=0).astype(BF16)
    grad_hidden = jnp.zeros((r, rows, width), F32)
    for k in range(r):
        swap = [
            (s * nv + t * r + h, t * nv + s * r + (h + k) % r)
            for s in range(nt)
            for t in range(nt)
            for h in range(r)
        ]
        piece = lax.dynamic_slice(coded, (0, lax.rem(part + k, r) * width), (rows + META, width))
        piece = lax.ppermute(piece, ("teacher", "vocab"), swap).astype(F32)
        piece = jnp.log2(piece[:rows]) * (piece[rows] * (1.0 / OCT))
        grad_hidden = lax.dynamic_update_slice(grad_hidden, piece[None], (lax.rem(part + r - k, r), 0, 0))
    return grad_hidden.reshape(r * rows, width)


def fused(nt, nv, tok, teacher_hidden, teacher_head, student_hidden, student_head):
    head, shead = teacher_head[0].T, student_head.T
    logits, stat, slog, columns = forward(teacher_hidden[0], head, student_hidden, shead, nv, 0)
    gradl, kl = combine(logits, stat, slog, nv, 1)
    every, gh, away, loss = gather(gradl, kl, shead, nv, 2)
    chips, rows = nv // 2, gh.shape[0]
    chip = lax.axis_index("vocab") // 2
    came = []
    for k in range(1, chips):
        piece = lax.dynamic_index_in_dim(away, lax.rem(chip + k, chips), 0, keepdims=False)
        came.append(lax.ppermute(piece, "vocab", [(i, (i + 2 * k) % nv) for i in range(nv)]))
    grad_weight = lax.dot_general(every, columns, (((1,), (0,)), ((), ())), preferred_element_type=F32)
    came, grad_weight = lax.optimization_barrier((came, grad_weight))
    for piece in came:
        piece = piece.astype(F32)
        gh = gh + jnp.log2(piece[:rows]) * (piece[rows] * (1.0 / OCT))
    return jnp.sum(loss[0]) / tok, spread_coded(nt, nv, gh, columns.shape[1]), grad_weight.T


def fits(nt, nv, tok, width):
    own = tok // nt
    return nt == 4 and nv == 2 * nt and own % 256 == 0 and width % (TURNS * META) == 0


def solution(mesh):
    nt, nv = mesh.shape["teacher"], mesh.shape["vocab"]

    def whole(teacher_hidden, teacher_head, student_hidden, student_head):
        tok = student_hidden.shape[0]
        step = fused if fits(nt, nv, tok, student_head.shape[1] // nv) else per_device
        return jax.shard_map(
            lambda *a: step(nt, nv, tok, *a),
            mesh=mesh,
            in_specs=(
                P("teacher", "vocab", None),
                P("teacher", None, "vocab"),
                P("teacher", None),
                P("teacher", "vocab"),
            ),
            out_specs=(P(), P("teacher", "vocab"), P("teacher", "vocab")),
            check_vma=False,
        )(teacher_hidden, teacher_head, student_hidden, student_head)

    return whole
```

```python
import functools

import jax
import jax.numpy as jnp
from jax import lax
from jax.experimental import pallas as pl
from jax.experimental.pallas import tpu as pltpu
from jax.sharding import PartitionSpec as P

F32 = jnp.float32
BF16 = jnp.bfloat16
MESH = pl.DeviceIdType.MESH
STEPS = 5
TURNS = 2 * STEPS
META = 16
OCT = 125.0
PIECES = 4
SLOTS = 5
AHEAD = 5


def fold(x, op):
    return op(x.reshape(x.shape[0] // 8, 8, x.shape[1]), axis=0)


def level(top):
    return (top * 1.01 + 1e-30).astype(BF16).astype(F32)


def push(src, dst, ssem, rsem, **to):
    return pltpu.make_async_remote_copy(
        src_ref=src, dst_ref=dst, send_sem=ssem, recv_sem=rsem, device_id=to, device_id_type=MESH
    )


def square():
    t = lax.axis_index("teacher")
    return t, t + 1 - 2 * lax.rem(t, 2), lax.rem(t + 2, 4), 3 - t


def sub_rows(rows):
    for n in (80, 64, 48, 32, 16):
        if rows % n == 0:
            return n


class Halving:
    def __init__(self, bufs, part):
        self.s1, self.r1, self.s2, self.r2, self.ss1, self.sr1, self.ss2, self.sr2 = bufs
        self.part = part
        self.sub = sub_rows(part)
        self.t, self.px, self.py, self.across = square()

    def near(self, i):
        return jnp.where(lax.rem(i, 2) == 0, self.px, self.py)

    def far(self, i):
        return jnp.where(lax.rem(i, 2) == 0, self.py, self.px)

    def first(self, i):
        return push(self.s1.at[i], self.r1.at[i], self.ss1.at[i], self.sr1.at[i], teacher=self.near(i))

    def second(self, i):
        return push(self.s2.at[i], self.r2.at[i], self.ss2.at[i], self.sr2.at[i], teacher=self.far(i))

    def meta(self, reach, c):
        hi = c.astype(BF16).astype(F32)
        mid = (c - hi).astype(BF16).astype(F32)
        lo = c - hi - mid
        row = lax.broadcasted_iota(jnp.int32, (META, c.shape[1]), 0)
        rows = jnp.where(row == 0, reach, jnp.where(row == 1, hi, jnp.where(row == 2, mid, lo)))
        return rows.astype(BF16)

    def read_meta(self, ref):
        m = ref[pl.ds(self.part, META), :].astype(F32)
        return m[0:1], m[1:2] + m[2:3] + m[3:4]

    def loop(self, body):
        def one(j, carry):
            body(pl.ds(pl.multiple_of(j * self.sub, self.sub), self.sub))
            return carry

        lax.fori_loop(0, self.part // self.sub, one, 0)

    def send(self, i, value, top, weight):
        for b, owner in enumerate((self.near(i), self.across)):
            reach = level(top(i, owner))
            rate = OCT / reach
            dst = self.s1.at[i, b]

            def body(rows):
                dst[rows, :] = jnp.exp2(value(i, owner, rows) * rate).astype(BF16)

            self.loop(body)
            dst[pl.ds(self.part, META), :] = self.meta(reach, weight(owner))
        self.first(i).start()

    def relay(self, i, value, top, weight):
        self.first(i).wait_recv()
        owner = self.far(i)
        src = self.r1.at[i, 1]
        dst = self.s2.at[i]
        r, c = self.read_meta(src)
        reach = level(r + top(i, owner))
        rate = OCT / reach
        back = r * (1.0 / OCT)

        def body(rows):
            y = jnp.log2(src[rows, :].astype(F32)) * back
            dst[rows, :] = jnp.exp2((value(i, owner, rows) + y) * rate).astype(BF16)

        self.loop(body)
        dst[pl.ds(self.part, META), :] = self.meta(reach, c + weight(owner))
        self.second(i).start()

    def finish(self, i, value, weight, emit):
        self.second(i).wait_recv()
        one, two = self.r1.at[i, 0], self.r2.at[i]
        r1, c1 = self.read_meta(one)
        r2, c2 = self.read_meta(two)
        k1, k2 = r1 * (1.0 / OCT), r2 * (1.0 / OCT)
        total = c1 + c2 + weight(self.t)

        def body(rows):
            y = jnp.log2(one[rows, :].astype(F32)) * k1
            z = jnp.log2(two[rows, :].astype(F32)) * k2
            emit(i, rows, value(i, self.t, rows) + y + z, total)

        self.loop(body)

    def drain(self):
        def one(i, carry):
            self.first(i).wait_send()
            self.second(i).wait_send()
            return carry

        lax.fori_loop(0, TURNS, one, 0)


def halving_scratch(part, own):
    sem = pltpu.SemaphoreType.DMA((TURNS,))
    one, two = (TURNS, 2, part + META, own), (TURNS, part + META, own)
    return [pltpu.VMEM(one, BF16)] * 2 + [pltpu.VMEM(two, BF16)] * 2 + [sem] * 4


def turn_row(i, width, part):
    return lax.rem(i, 2) * (width // 2) + i // 2 * part


NT = (((1,), (1,)), ((), ()))


def forward_kernel(chips, th, head, sh, shead, logits, stat, slog, cols, *scratch):
    halving = Halving(scratch[:8], head.shape[0] // TURNS)
    (hid, wbuf, ws, work, tops, ends, acc, wsem, vsem, lsem, outsem, zs, zr, cs, cr, os_, or_, fs, fr, gs, gr) = scratch[8:]
    width = head.shape[0]
    part = width // TURNS
    rows = th.shape[0]
    piece = rows // PIECES
    feats = ws.shape[2]
    own = sh.shape[0]
    hops = chips - 1
    tiles = TURNS
    t = halving.t
    v = lax.axis_index("vocab")
    core = lax.rem(v, 2)
    chip = v // 2
    twin = v + 1 - 2 * core
    others = (halving.px, halving.py, halving.across)

    barrier = pltpu.get_barrier_semaphore()
    for p in others:
        pl.semaphore_signal(barrier, inc=1, device_id={"teacher": p}, device_id_type=MESH)
    pl.semaphore_signal(barrier, inc=1, device_id={"vocab": twin}, device_id_type=MESH)

    @pl.when(chip > 0)
    def _():
        pl.semaphore_signal(barrier, inc=1, device_id={"vocab": v - 2}, device_id_type=MESH)

    @pl.when(chip < chips - 1)
    def _():
        pl.semaphore_signal(barrier, inc=1, device_id={"vocab": v + 2}, device_id_type=MESH)

    def tile_copy(g):
        slot = lax.rem(g, AHEAD)
        at = pl.ds(pl.multiple_of(lax.rem(g, tiles) * part, part), part)
        return pltpu.make_async_copy(head.at[at], wbuf.at[slot], wsem.at[slot])

    def lanes(n):
        return pl.ds(pl.multiple_of(n * feats, feats), feats)

    def block(s, c):
        return pl.ds(pl.multiple_of((s * 2 + c) * rows, rows), rows)

    own_hid = pltpu.make_async_copy(th, hid.at[block(chip, core)], lsem.at[0])
    own_cols = pltpu.make_async_copy(sh.at[:, lanes(t)], cols.at[pl.ds(pl.multiple_of(t * own, own), own)], lsem.at[1])

    def ws_copy(i):
        at = pl.ds(pl.multiple_of(turn_row(i, width, part), META), part)
        return pltpu.make_async_copy(shead.at[at], ws.at[lax.rem(i, 2)], vsem.at[lax.rem(i, 2)])

    own_hid.start()
    for g in range(AHEAD - 1):
        tile_copy(g).start()
    own_cols.start()
    ws_copy(0).start()

    @pl.when((chip > 0) & (chip < chips - 1))
    def _():
        pl.semaphore_wait(barrier, 6)

    @pl.when((chip == 0) | (chip == chips - 1))
    def _():
        pl.semaphore_wait(barrier, 5)

    half = own // 2

    def col_rows(owner):
        return pl.ds(pl.multiple_of(owner * own + core * half, half), half)

    def col_out(n):
        src = sh.at[pl.ds(pl.multiple_of(core * half, half), half), lanes(others[n])]
        return push(src, cols.at[col_rows(t)], fs.at[n], fr.at[n], teacher=others[n])

    def col_twin(n):
        at = cols.at[col_rows(others[n])]
        return push(at, at, gs.at[n], gr.at[n], vocab=twin)

    for n in range(3):
        col_out(n).start()

    twin_own = push(th, hid.at[block(chip, core)], os_.at[0], or_.at[0], vocab=twin)
    twin_own.start()

    def at(s, q):
        return hid.at[pl.ds(pl.multiple_of((s * 2 + core) * rows + q * piece, piece), piece)]

    def along(d, h, q):
        s = chip - h if d == 0 else chip + h
        return push(at(s, q), at(s, q), zs.at[d, h, q], zr.at[d, h, q], vocab=v + 2 if d == 0 else v - 2)

    def arrived(d, h, q):
        s = chip - 1 - h if d == 0 else chip + 1 + h
        return push(at(s, q), at(s, q), zs.at[d, h, q], zr.at[d, h, q], vocab=v + 2 if d == 0 else v - 2)

    def across(d, h, q):
        s = chip - 1 - h if d == 0 else chip + 1 + h
        return push(at(s, q), at(s, q), cs.at[d, h, q], cr.at[d, h, q], vocab=twin)

    def arrives(d, h):
        return chip - 1 - h >= 0 if d == 0 else chip + 1 + h <= chips - 1

    def sends(d, h):
        return (chip - h >= 0) & (chip + 1 <= chips - 1) if d == 0 else (chip + h <= chips - 1) & (chip >= 1)

    own_hid.wait()
    for d in range(2):

        @pl.when(sends(d, 0))
        def _():
            for q in range(PIECES):
                along(d, 0, q).start()

    def event(j, carry):
        h = j // PIECES
        q = lax.rem(j, PIECES)
        for d in range(2):

            @pl.when(arrives(d, h))
            def _():
                arrived(d, h, q).wait_recv()
                across(d, h, q).start()

            @pl.when(arrives(d, h) & sends(d, h + 1))
            def _():
                along(d, h + 1, q).start()

        return carry

    short = jnp.minimum(chip, chips - 1 - chip)

    def source(p):
        d = (p + 1) // 2
        near = jnp.where(lax.rem(p, 2) == 1, chip - d, chip + d)
        beyond = jnp.where(chip == short, chip + p - short, chip - p + short)
        return jnp.where(p <= 2 * short, near, beyond)

    def flush(s):
        return pltpu.make_async_copy(acc, logits.at[s], outsem.at[0])

    def tile(g, carry):
        p = g // tiles
        kt = lax.rem(g, tiles)
        s = source(p)

        @pl.when(g + AHEAD - 1 < chips * tiles)
        def _():
            tile_copy(g + AHEAD - 1).start()

        @pl.when(kt == 0)
        def _():
            @pl.when(p == 0)
            def _():
                twin_own.wait_recv()

            for d in range(2):

                @pl.when((s < chip) if d == 0 else (s > chip))
                def _():
                    h = (chip - s if d == 0 else s - chip) - 1
                    for q in range(PIECES):
                        across(d, h, q).wait_recv()

            @pl.when(p > 0)
            def _():
                flush(0).wait()

            big = jnp.full((8, 2 * rows), 3e38, F32)
            ends[0] = -big
            ends[1] = big

        tile_copy(g).wait()
        a = hid[pl.ds(pl.multiple_of(s * 2 * rows, 2 * rows), 2 * rows), :]
        x = lax.dot_general(wbuf[lax.rem(g, AHEAD)], a, NT, preferred_element_type=F32)
        acc[pl.ds(pl.multiple_of(kt * part, part), part), :] = x
        ends[0] = jnp.maximum(ends[0], fold(x, jnp.max))
        ends[1] = jnp.minimum(ends[1], fold(x, jnp.min))

        @pl.when(kt == tiles - 1)
        def _():
            flush(s).start()
            sub = halving.sub
            n = 2 * rows

            m = jnp.max(ends[0], axis=0, keepdims=True)

            def sums(j, c):
                x = acc[pl.ds(pl.multiple_of(j * sub, sub), sub), :]
                e = jnp.exp(x - m)
                return c[0] + fold(e, jnp.sum), c[1] + fold(e * x, jnp.sum)

            zero = jnp.zeros((8, n), F32)
            z, f = lax.fori_loop(0, width // sub, sums, (zero, zero))
            z, f = jnp.sum(z, axis=0, keepdims=True), jnp.sum(f, axis=0, keepdims=True)
            low = jnp.min(ends[1], axis=0, keepdims=True)
            row = lax.broadcasted_iota(jnp.int32, (8, n), 0)
            stat[s] = jnp.where(row == 0, m, jnp.where(row == 1, z, jnp.where(row == 2, f, low)))

        return carry

    lax.fori_loop(0, tiles - 2, tile, 0)
    for n in range(3):
        col_out(n).wait_recv()
        col_twin(n).start()
    lax.fori_loop(tiles - 2, tiles, tile, 0)
    for n in range(3):
        col_twin(n).wait_recv()
    own_cols.wait()

    def value(i, owner, r):
        return work[lax.rem(i, SLOTS), owner, r, :]

    def top(i, owner):
        return jnp.max(tops[lax.rem(i, SLOTS), owner], axis=0, keepdims=True)

    def weight(owner):
        return jnp.ones((1, own), F32)

    def emit(i, r, x, c):
        slog[pl.ds(pl.multiple_of(turn_row(i, width, part) + r.start, halving.sub), halving.sub), :] = x

    events = hops * PIECES

    def seen(i):
        return jnp.where(i < 0, 0, jnp.minimum(2 + 6 * jnp.maximum(i, 0) // 5, events))

    def done(i):
        one = jnp.minimum(tiles + 4 * jnp.maximum(i - 1, 0), 2 * tiles)
        two = jnp.minimum(2 * tiles + 3 * jnp.maximum(i - 4, 0), 3 * tiles)
        three = jnp.minimum(3 * tiles + 4 * jnp.maximum(i - 8, 0), 4 * tiles)
        return jnp.where(i < 5, one, jnp.where(i < 9, two, three))

    def turn(i, carry):
        lax.fori_loop(seen(i - 1), seen(i), event, 0)

        @pl.when(i < TURNS)
        def _():
            @pl.when(i + 1 < TURNS)
            def _():
                ws_copy(i + 1).start()

            ws_copy(i).wait()
            a = ws[lax.rem(i, 2)]
            for owner in range(4):
                x = lax.dot_general(a, cols[pl.ds(owner * own, own), :], NT, preferred_element_type=F32)
                work[lax.rem(i, SLOTS), owner] = x
                tops[lax.rem(i, SLOTS), owner] = fold(jnp.abs(x), jnp.max)
            halving.send(i, value, top, weight)

        @pl.when((i >= 2) & (i < TURNS + 2))
        def _():
            halving.relay(i - 2, value, top, weight)

        @pl.when(i >= 4)
        def _():
            halving.finish(i - 4, value, weight, emit)

        lax.fori_loop(done(i - 1), done(i), tile, 0)
        return carry

    lax.fori_loop(0, TURNS + 4, turn, 0)

    flush(0).wait()
    halving.drain()
    for n in range(3):
        col_out(n).wait_send()
        col_twin(n).wait_send()
    twin_own.wait_send()

    def sent(j, carry):
        h = j // PIECES
        q = lax.rem(j, PIECES)
        for d in range(2):

            @pl.when(sends(d, h))
            def _():
                along(d, h, q).wait_send()

            @pl.when(arrives(d, h))
            def _():
                across(d, h, q).wait_send()

        return carry

    lax.fori_loop(0, events, sent, 0)


def forward(th, head, sh, shead, nv, ident):
    chips = nv // 2
    rows, depth = th.shape
    width = head.shape[0]
    feats = shead.shape[1]
    own = sh.shape[0]
    part = width // TURNS
    hops = chips - 1
    hbm = pl.BlockSpec(memory_space=pl.ANY)
    vmem = pl.BlockSpec(memory_space=pltpu.VMEM)
    dma = pltpu.SemaphoreType.DMA
    relays = dma((2, hops, PIECES))
    return pl.pallas_call(
        functools.partial(forward_kernel, chips),
        out_shape=(
            jax.ShapeDtypeStruct((chips, width, 2 * rows), F32),
            jax.ShapeDtypeStruct((chips, 8, 2 * rows), F32),
            jax.ShapeDtypeStruct((width, own), F32),
            jax.ShapeDtypeStruct((4 * own, feats), BF16),
        ),
        in_specs=[hbm] * 4,
        out_specs=(hbm, vmem, vmem, vmem),
        scratch_shapes=halving_scratch(part, own)
        + [
            pltpu.VMEM((nv * rows, depth), BF16),
            pltpu.VMEM((AHEAD, part, depth), BF16),
            pltpu.VMEM((2, part, feats), BF16),
            pltpu.VMEM((SLOTS, 4, part, own), F32),
            pltpu.VMEM((SLOTS, 4, 8, own), F32),
            pltpu.VMEM((2, 8, 2 * rows), F32),
            pltpu.VMEM((width, 2 * rows), F32),
            dma((AHEAD,)),
            dma((2,)),
            dma((2,)),
            dma((1,)),
            relays,
            relays,
            relays,
            relays,
            dma((1,)),
            dma((1,)),
            dma((3,)),
            dma((3,)),
            dma((3,)),
            dma((3,)),
        ],
        compiler_params=pltpu.CompilerParams(
            collective_id=ident, has_side_effects=True, vmem_limit_bytes=60 * 2**20
        ),
        name="forward",
    )(th, head, sh, shead)


def combine_kernel(nv, logits, stat, slog, grad, kl, *scratch):
    width, own = slog.shape
    part = width // TURNS
    halving = Halving(scratch[:8], part)
    lg, raw, peak, st, mine, st2, lsem, ssem, rsem, ssem2, rsem2 = scratch[8:]
    t = halving.t
    v = lax.axis_index("vocab")
    sub = halving.sub

    def fetch(n, owner):
        return pltpu.make_async_copy(logits.at[owner], lg.at[owner], lsem.at[n])

    order = (halving.px, halving.across, halving.py, t)
    for n in range(4):
        fetch(n, order[n]).start()

    barrier = pltpu.get_barrier_semaphore()
    for p in (halving.px, halving.py):
        pl.semaphore_signal(barrier, inc=1, device_id={"teacher": p}, device_id_type=MESH)
    for n in range(1, nv):
        pl.semaphore_signal(barrier, inc=1, device_id={"vocab": lax.rem(v + n, nv)}, device_id_type=MESH)
    pl.semaphore_wait(barrier, nv + 1)

    def share(n, src, dst, ss, rs):
        return push(src, dst.at[v], ss.at[n - 1], rs.at[n - 1], vocab=lax.rem(v + n, nv))

    for n in range(1, nv):
        share(n, stat, st, ssem, rsem).start()
    st[v] = stat[...]

    zero = jnp.zeros((8, own), F32)

    def at(j):
        return pl.ds(pl.multiple_of(j * sub, sub), sub)

    def student():
        m = lax.fori_loop(0, width // sub, lambda j, c: jnp.maximum(c, fold(slog[at(j), :], jnp.max)), zero - 3e38)
        m = jnp.max(m, axis=0, keepdims=True)
        z = lax.fori_loop(0, width // sub, lambda j, c: c + fold(jnp.exp(slog[at(j), :] - m), jnp.sum), zero)
        peak[1] = jnp.broadcast_to(m, (8, own))
        peak[2] = z

    for n in range(1, nv):
        share(n, stat, st, ssem, rsem).wait()

    for o in range(4):
        m = [st[s, o, 0:1, :] for s in range(nv)]
        big = functools.reduce(jnp.maximum, m)
        scale = [jnp.exp(x - big) for x in m]
        total = sum(st[s, o, 1:2, :] * scale[s] for s in range(nv))
        moment = sum(st[s, o, 2:3, :] * scale[s] for s in range(nv))
        lse = big + jnp.log(total)
        conf = jnp.exp(moment / total - lse)
        reach = conf * jnp.maximum(jnp.abs(stat[o, 0:1, :] - lse), jnp.abs(stat[o, 3:4, :] - lse))
        row = lax.broadcasted_iota(jnp.int32, (8, own), 0)
        mine[o] = jnp.where(row == 0, conf, jnp.where(row == 1, lse, reach))
    for n in range(2):
        fetch(n, order[n]).wait()

    def value(i, owner, r):
        rows = pl.ds(pl.multiple_of(turn_row(i, width, part) + r.start, sub), sub)
        return mine[owner, 0:1, :] * (lg[owner, rows, :] - mine[owner, 1:2, :])

    def top(i, owner):
        return mine[owner, 2:3, :]

    def weight(owner):
        return mine[owner, 0:1, :]

    peak[0] = zero - 3e38

    def emit(i, r, x, c):
        rows = pl.ds(pl.multiple_of(turn_row(i, width, part) + r.start, sub), sub)
        x = x * (1.0 / c)
        raw[rows, :] = x
        peak[0] = jnp.maximum(peak[0], fold(x, jnp.max))

    def turn(i, carry):
        for n in (2, 3):

            @pl.when(i == n - 2)
            def _():
                fetch(n, order[n]).wait()

        @pl.when(2 * i < TURNS)
        def _():
            halving.send(2 * i, value, top, weight)
            halving.send(2 * i + 1, value, top, weight)

        @pl.when(i == 1)
        def _():
            student()

        @pl.when((i >= 2) & (i < TURNS + 2))
        def _():
            halving.relay(i - 2, value, top, weight)

        @pl.when(i >= 4)
        def _():
            halving.finish(i - 4, value, weight, emit)

        return carry

    lax.fori_loop(0, TURNS + 4, turn, 0)

    mr = jnp.max(peak[0], axis=0, keepdims=True)
    ms = peak[1, 0:1]
    ss = jnp.sum(peak[2], axis=0, keepdims=True)

    def sums(j, c):
        x = raw[at(j), :]
        e = jnp.exp(x - mr)
        return c[0] + fold(e, jnp.sum), c[1] + fold(e * (x - slog[at(j), :]), jnp.sum)

    sr, cross = lax.fori_loop(0, width // sub, sums, (zero, zero))
    sr, cross = jnp.sum(sr, axis=0, keepdims=True), jnp.sum(cross, axis=0, keepdims=True)
    row = lax.broadcasted_iota(jnp.int32, (8, own), 0)
    mine[0] = jnp.where(
        row == 0, mr, jnp.where(row == 1, sr, jnp.where(row == 2, cross, jnp.where(row == 3, ms, ss)))
    )
    for n in range(1, nv):
        share(n, mine.at[0], st2, ssem2, rsem2).start()
    st2[v] = mine[0]
    halving.drain()
    for n in range(1, nv):
        share(n, mine.at[0], st2, ssem2, rsem2).wait()
    every = [st2[s] for s in range(nv)]
    tr = functools.reduce(jnp.maximum, [x[0:1] for x in every])
    ts = functools.reduce(jnp.maximum, [x[3:4] for x in every])
    cr = [jnp.exp(x[0:1] - tr) for x in every]
    total_r = sum(x[1:2] * c for x, c in zip(every, cr))
    cross = sum(x[2:3] * c for x, c in zip(every, cr))
    total_s = sum(x[4:5] * jnp.exp(x[3:4] - ts) for x in every)
    lse_r = tr + jnp.log(total_r)
    lse_s = ts + jnp.log(total_s)
    kl[...] = jnp.broadcast_to(cross / total_r - lse_r + lse_s, (8, own))

    def grads(j, c):
        grad[at(j), :] = (jnp.exp(slog[at(j), :] - lse_s) - jnp.exp(raw[at(j), :] - lse_r)).astype(BF16)
        return c

    lax.fori_loop(0, width // sub, grads, 0)


def combine(logits, stat, slog, nv, ident):
    width, own = slog.shape
    part = width // TURNS
    hbm = pl.BlockSpec(memory_space=pl.ANY)
    vmem = pl.BlockSpec(memory_space=pltpu.VMEM)
    dma = pltpu.SemaphoreType.DMA
    return pl.pallas_call(
        functools.partial(combine_kernel, nv),
        out_shape=(jax.ShapeDtypeStruct((width, own), BF16), jax.ShapeDtypeStruct((8, own), F32)),
        in_specs=[hbm, vmem, vmem],
        out_specs=(vmem, vmem),
        scratch_shapes=halving_scratch(part, own)
        + [
            pltpu.VMEM((4, width, own), F32),
            pltpu.VMEM((width, own), F32),
            pltpu.VMEM((3, 8, own), F32),
            pltpu.VMEM((nv, 4, 8, own), F32),
            pltpu.VMEM((4, 8, own), F32),
            pltpu.VMEM((nv, 8, own), F32),
            dma((4,)),
            dma((nv - 1,)),
            dma((nv - 1,)),
            dma((nv - 1,)),
            dma((nv - 1,)),
        ],
        compiler_params=pltpu.CompilerParams(
            collective_id=ident, has_side_effects=True, vmem_limit_bytes=60 * 2**20
        ),
        name="combine",
    )(logits, stat, slog)


def spread(nt, nv, gh, feats):
    r = nv // nt
    part = lax.rem(lax.axis_index("vocab"), r)
    rows, width = gh.shape[0], feats // r
    grad_hidden = jnp.zeros((r, rows, width), F32)
    for k in range(r):
        swap = [
            (s * nv + t * r + h, t * nv + s * r + (h + k) % r)
            for s in range(nt)
            for t in range(nt)
            for h in range(r)
        ]
        piece = lax.dynamic_slice(gh, (0, lax.rem(part + k, r) * width), (rows, width))
        piece = lax.ppermute(piece, ("teacher", "vocab"), swap)
        grad_hidden = lax.dynamic_update_slice(
            grad_hidden, piece[None], (lax.rem(part + r - k, r), 0, 0)
        )
    return grad_hidden.reshape(r * rows, width)


def gather_hidden(own, nv, first):
    chips = nv // 2
    at = lax.axis_index("vocab")
    chip = at // 2
    up = [own]
    down = [own]
    for hop in range(chips - 1):
        up.append(lax.ppermute(up[-1], "vocab", [(i, i + 2) for i in range(nv - 2)]))
        down.append(lax.ppermute(down[-1], "vocab", [(i + 2, i) for i in range(nv - 2)]))
        if hop == 1:
            up[-1], down[-1], first = lax.optimization_barrier((up[-1], down[-1], first))
    pair = [(i, i ^ 1) for i in range(nv)]
    rows, width = own.shape
    buf = jnp.zeros((chips, 2, rows, width), own.dtype)
    core = at % 2
    for k in range(chips):
        piece = own if k == 0 else up[k] + down[chips - k]
        other = lax.ppermute(piece, "vocab", pair)
        slot = lax.rem(chip - k + chips, chips)
        buf = lax.dynamic_update_slice(buf, piece[None, None], (slot, core, 0, 0))
        buf = lax.dynamic_update_slice(buf, other[None, None], (slot, 1 - core, 0, 0))
    return buf.reshape(nv * rows, width), first


def exchange_kernel(nv, own_ref, out_ref, slots, send, recv):
    me = lax.axis_index("vocab")
    barrier = pltpu.get_barrier_semaphore()
    for step in range(1, nv):
        pl.semaphore_signal(
            barrier,
            inc=1,
            device_id={"vocab": lax.rem(me + step, nv)},
            device_id_type=pl.DeviceIdType.MESH,
        )
    pl.semaphore_wait(barrier, nv - 1)
    copies = []
    for step in range(1, nv):
        copies.append(
            pltpu.make_async_remote_copy(
                src_ref=own_ref,
                dst_ref=slots.at[me],
                send_sem=send.at[step - 1],
                recv_sem=recv.at[step - 1],
                device_id={"vocab": lax.rem(me + step, nv)},
                device_id_type=pl.DeviceIdType.MESH,
            )
        )
        copies[-1].start()
    slots[me] = own_ref[...]
    for copy in copies:
        copy.wait()
    out_ref[...] = slots[...]


def slotted(stats, nv, ident):
    return pl.pallas_call(
        functools.partial(exchange_kernel, nv),
        out_shape=jax.ShapeDtypeStruct((nv,) + stats.shape, F32),
        in_specs=[pl.BlockSpec(memory_space=pltpu.VMEM)],
        out_specs=pl.BlockSpec(memory_space=pltpu.VMEM),
        scratch_shapes=[
            pltpu.VMEM((nv,) + stats.shape, F32),
            pltpu.SemaphoreType.DMA((nv - 1,)),
            pltpu.SemaphoreType.DMA((nv - 1,)),
        ],
        compiler_params=pltpu.CompilerParams(collective_id=ident, has_side_effects=True),
    )(stats)


def per_device(nt, nv, tok, teacher_hidden, teacher_head, student_hidden, student_head):
    head = teacher_head[0]
    columns = lax.all_to_all(student_hidden, "teacher", split_axis=1, concat_axis=0, tiled=True)
    partial_slog = jnp.dot(columns, student_head, preferred_element_type=F32)
    hidden, partial_slog = gather_hidden(teacher_hidden[0], nv, partial_slog)
    slog = lax.psum_scatter(partial_slog, "teacher", scatter_dimension=0, tiled=True)

    logits = jnp.dot(hidden, head, preferred_element_type=F32)
    m = jnp.max(logits, axis=-1)
    e = jnp.exp(logits - m[:, None])
    st = slotted(jnp.stack([m, jnp.sum(e, axis=-1), jnp.sum(e * logits, axis=-1)]), nv, 0)
    top = jnp.max(st[:, 0], axis=0)
    scale = jnp.exp(st[:, 0] - top)
    total = jnp.sum(st[:, 1] * scale, axis=0)
    moment = jnp.sum(st[:, 2] * scale, axis=0)
    lse = top + jnp.log(total)
    confid = jnp.exp(moment / total - lse)
    weighted = confid[:, None] * (logits - lse[:, None])
    slog, weighted = lax.optimization_barrier((slog, weighted))
    wsum = lax.psum_scatter(weighted, "teacher", scatter_dimension=0, tiled=True)
    csum = lax.psum_scatter(confid, "teacher", scatter_dimension=0, tiled=True)

    raw = wsum / csum[:, None]
    ms = jnp.max(slog, axis=-1)
    ss = jnp.sum(jnp.exp(slog - ms[:, None]), axis=-1)
    mr = jnp.max(raw, axis=-1)
    er = jnp.exp(raw - mr[:, None])
    st = slotted(
        jnp.stack([mr, jnp.sum(er, axis=-1), jnp.sum(er * (raw - slog), axis=-1), ms, ss]), nv, 1
    )
    tr = jnp.max(st[:, 0], axis=0)
    cr = jnp.exp(st[:, 0] - tr)
    total_r = jnp.sum(st[:, 1] * cr, axis=0)
    cross = jnp.sum(st[:, 2] * cr, axis=0)
    ts = jnp.max(st[:, 3], axis=0)
    total_s = jnp.sum(st[:, 4] * jnp.exp(st[:, 3] - ts), axis=0)
    lse_r = tr + jnp.log(total_r)
    lse_s = ts + jnp.log(total_s)
    kl = cross / total_r - lse_r + lse_s
    gradl = (jnp.exp(slog - lse_s[:, None]) - jnp.exp(raw - lse_r[:, None])).astype(jnp.bfloat16)
    all_grads = lax.all_gather(gradl, "teacher", axis=0, tiled=True)
    loss = lax.psum(jnp.sum(kl), "teacher") / tok
    all_grads, loss = lax.optimization_barrier((all_grads, loss))

    feats = student_head.shape[0]
    gh = lax.dot_general(
        all_grads, student_head, (((1,), (1,)), ((), ())), preferred_element_type=F32
    )
    gh = lax.psum_scatter(gh, "vocab", scatter_dimension=0, tiled=True)
    grad_weight = lax.dot_general(
        columns, all_grads, (((0,), (0,)), ((), ())), preferred_element_type=F32
    )
    gh, grad_weight = lax.optimization_barrier((gh, grad_weight))
    return loss, spread(nt, nv, gh, feats), grad_weight


def gather_kernel(nv, grad, kl, shead, every, mine, away, first, loss, *scratch):
    g, ws, gh, rx, came, fin, sums, a_s, a_r, b_s, b_r, c_s, c_r, x_s, x_r, z_s, z_r, p_s, p_r, l_s, l_r, lsem, fsem = scratch
    width, own = grad.shape
    feats = ws.shape[1]
    part = width // TURNS
    rows = 4 * own // nv
    chips = nv // 2
    t, px, py, diagonal = square()
    v = lax.axis_index("vocab")
    core = lax.rem(v, 2)
    chip = v // 2
    twin = v + 1 - 2 * core
    own_ws = pltpu.make_async_copy(shead, ws, lsem.at[0])
    own_ws.start()

    half = own // 2

    def span(i):
        return pl.ds(pl.multiple_of(turn_row(lax.rem(i, TURNS), width, part), META), part)

    def lanes(owner, i):
        return pl.ds(pl.multiple_of(owner * own + i // TURNS * half, half), half)

    def source(i):
        return grad.at[span(i), pl.ds(pl.multiple_of(i // TURNS * half, half), half)]

    own_g = pltpu.make_async_copy(grad, g.at[:, pl.ds(pl.multiple_of(t * own, own), own)], lsem.at[1])
    own_g.start()
    barrier = pltpu.get_barrier_semaphore()
    for p in (px, py, diagonal):
        pl.semaphore_signal(barrier, inc=1, device_id={"teacher": p}, device_id_type=MESH)
    pl.semaphore_signal(barrier, inc=1, device_id={"vocab": twin}, device_id_type=MESH)
    for k in range(1, chips):
        pl.semaphore_signal(barrier, inc=1, device_id={"vocab": lax.rem(v + 2 * k, nv)}, device_id_type=MESH)

    def goal(h):
        return {"teacher": chip, "vocab": 2 * t + h}

    here = (chip == t) & (core == 0)

    @pl.when(jnp.logical_not(here))
    def _():
        pl.semaphore_signal(barrier, inc=1, device_id={"teacher": chip, "vocab": 2 * t}, device_id_type=MESH)

    @pl.when(core == 1)
    def _():
        pl.semaphore_wait(barrier, chips + 3)

    @pl.when((core == 0) & (chip != t))
    def _():
        pl.semaphore_wait(barrier, chips + 5)

    @pl.when(here)
    def _():
        pl.semaphore_wait(barrier, chips + 4)

    def deliver(h):
        return push(fin.at[h], first, p_s.at[h], p_r.at[0], **goal(h))

    def stay():
        return pltpu.make_async_copy(fin.at[0], first, p_s.at[0])

    def near(i):
        return jnp.where(lax.rem(i, 2) == 0, px, py)

    def far(i):
        return jnp.where(lax.rem(i, 2) == 0, py, px)

    def to_near(i):
        return push(source(i), g.at[span(i), lanes(t, i)], a_s.at[i], a_r.at[i], teacher=near(i))

    def to_far(i):
        return push(source(i), g.at[span(i), lanes(t, i)], b_s.at[i], b_r.at[i], teacher=far(i))

    def onward(i):
        at = g.at[span(i), lanes(near(i), i)]
        return push(at, at, c_s.at[i], c_r.at[i], teacher=far(i))

    def keep(i):
        return pltpu.make_async_copy(g.at[span(i)], every.at[span(i)], fsem.at[lax.rem(i, TURNS)])

    to_near(0).start()
    to_far(0).start()

    x = kl[...]
    lane = 128
    part_sum = sum(x[:, n * lane : (n + 1) * lane] for n in range(own // lane))
    sums[t] = part_sum
    others = (px, py, diagonal)

    def tell(n):
        return push(sums.at[t], sums.at[t], l_s.at[n], l_r.at[n], teacher=others[n])

    for n in range(3):
        tell(n).start()
    gh[...] = jnp.zeros_like(gh)
    own_ws.wait()
    own_g.wait()

    def swap(c):
        src = gh.at[pl.ds(pl.multiple_of((2 * c + 1 - core) * rows, rows), rows)]
        return push(src, rx.at[c], x_s.at[c], x_r.at[c], vocab=twin)

    def along(c):
        return push(away.at[c], came.at[chip], z_s.at[c], z_r.at[chip], vocab=2 * c + core)

    def arrived(c):
        return push(away.at[c], came.at[c], z_s.at[c], z_r.at[c], vocab=2 * c + core)

    def settle():
        for c in range(chips):
            swap(c).wait_recv()
            for f in range(feats // own):
                cut = pl.ds(f * own, own)
                x = gh[pl.ds(pl.multiple_of((2 * c + core) * rows, rows), rows), cut] + rx[c, :, cut]
                reach = level(jnp.max(fold(jnp.abs(x), jnp.max), axis=0, keepdims=True))
                away[c, pl.ds(0, rows), cut] = jnp.exp2(x * (OCT / reach)).astype(BF16)
                away[c, pl.ds(rows, META), cut] = jnp.broadcast_to(reach, (META, own)).astype(BF16)

                @pl.when(chip == c)
                def _():
                    mine[:, cut] = x

    def reduced():
        for c in range(chips):

            @pl.when(chip != c)
            def _():
                arrived(c).wait_recv()

        for f in range(feats // own):
            cut = pl.ds(f * own, own)
            x = mine[:, cut]
            for k in range(1, chips):
                other = came.at[lax.rem(chip + k, chips)]
                back = other[pl.ds(rows, META), cut].astype(F32)[0:1] * (1.0 / OCT)
                x = x + jnp.log2(other[pl.ds(0, rows), cut].astype(F32)) * back
            reach = level(jnp.max(fold(jnp.abs(x), jnp.max), axis=0, keepdims=True))
            h, at = f * own // (feats // 2), f * own % (feats // 2)
            fin[h, pl.ds(0, rows), pl.ds(at, own)] = jnp.exp2(x * (OCT / reach)).astype(BF16)
            fin[h, pl.ds(rows, META), pl.ds(at, own)] = jnp.broadcast_to(reach, (META, own)).astype(BF16)

        @pl.when(chip != t)
        def _():
            deliver(0).start()

        @pl.when(chip == t)
        def _():
            stay().start()

        deliver(1).start()

    def turn(i, carry):
        @pl.when(i + 1 < 2 * TURNS)
        def _():
            to_near(i + 1).start()
            to_far(i + 1).start()

        @pl.when(i < 2 * TURNS)
        def _():
            to_near(i).wait_recv()
            onward(i).start()

        @pl.when((i == TURNS + 4) & (core == 0))
        def _():
            settle()
            for c in range(chips):

                @pl.when(chip != c)
                def _():
                    along(c).start()

        @pl.when(i >= 2)
        def _():
            k = i - 2
            to_far(k).wait_recv()
            onward(k).wait_recv()

            @pl.when(k >= TURNS)
            def _():
                keep(k).start()

            a = jnp.concatenate([g[span(k), lanes(owner, k)] for owner in range(4)], axis=1)
            for f in range(feats // own):
                cut = pl.ds(f * own, own)
                x = lax.dot_general(a, ws[span(k), cut], (((0,), (0,)), ((), ())), preferred_element_type=F32)
                for owner in range(4):
                    at = pl.ds(pl.multiple_of(owner * own + k // TURNS * half, half), half)
                    gh[at, cut] += x[owner * half : (owner + 1) * half]

        @pl.when((i == 2 * TURNS - 1) & (core == 0))
        def _():
            reduced()

        @pl.when((i == TURNS + 1) & (core == 1))
        def _():
            for c in range(chips):
                swap(c).start()

        return carry

    lax.fori_loop(0, 2 * TURNS + 2, turn, 0)

    @pl.when(core == 0)
    def _():
        for c in range(chips):
            swap(c).start()

    for n in range(3):
        tell(n).wait()
    loss[...] = sums[0] + sums[1] + sums[2] + sums[3]

    @pl.when(core == 1)
    def _():
        settle()

    @pl.when(core == 0)
    def _():
        for c in range(chips):

            @pl.when(chip != c)
            def _():
                along(c).wait_send()

        deliver(1).wait_send()

        @pl.when(chip != t)
        def _():
            deliver(0).wait_send()

        @pl.when(chip == t)
        def _():
            stay().wait()

    @pl.when(jnp.logical_not(here))
    def _():
        deliver(0).wait_recv()

    for c in range(chips):
        swap(c).wait_send()

    def drain(i, carry):
        to_near(i).wait_send()
        to_far(i).wait_send()
        onward(i).wait_send()

        @pl.when(i >= TURNS)
        def _():
            keep(i).wait()

        return carry

    lax.fori_loop(0, 2 * TURNS, drain, 0)


def gather(grad, kl, shead, nv, ident):
    width, own = grad.shape
    feats = shead.shape[1]
    chips = nv // 2
    rows = 4 * own // nv
    hbm = pl.BlockSpec(memory_space=pl.ANY)
    vmem = pl.BlockSpec(memory_space=pltpu.VMEM)
    dma = pltpu.SemaphoreType.DMA
    return pl.pallas_call(
        functools.partial(gather_kernel, nv),
        out_shape=(
            jax.ShapeDtypeStruct((width, 4 * own), BF16),
            jax.ShapeDtypeStruct((rows, feats), F32),
            jax.ShapeDtypeStruct((chips, rows + META, feats), BF16),
            jax.ShapeDtypeStruct((rows + META, feats // 2), BF16),
            jax.ShapeDtypeStruct((8, 128), F32),
        ),
        in_specs=[vmem, vmem, hbm],
        out_specs=(hbm, vmem, vmem, vmem, vmem),
        scratch_shapes=[
            pltpu.VMEM((width, 4 * own), BF16),
            pltpu.VMEM((width, feats), BF16),
            pltpu.VMEM((4 * own, feats), F32),
            pltpu.VMEM((chips, rows, feats), F32),
            pltpu.VMEM((chips, rows + META, feats), BF16),
            pltpu.VMEM((2, rows + META, feats // 2), BF16),
            pltpu.VMEM((4, 8, 128), F32),
        ]
        + [dma((2 * TURNS,))] * 6
        + [dma((chips,))] * 4
        + [dma((2,))] * 2
        + [dma((3,))] * 2
        + [dma((2,)), dma((TURNS,))],
        compiler_params=pltpu.CompilerParams(
            collective_id=ident, has_side_effects=True, vmem_limit_bytes=56 * 2**20
        ),
        name="gather",
    )(grad, kl, shead)


def decoded(piece):
    piece = piece.astype(F32)
    rows = piece.shape[0] - META
    return jnp.log2(piece[:rows]) * (piece[rows] * (1.0 / OCT))


def place(nt, nv, gh, h):
    core = lax.rem(lax.axis_index("vocab"), 2)
    rows, feats = gh.shape
    reach = lax.reduce_precision(jnp.max(jnp.abs(gh), axis=0, keepdims=True) * 1.01 + 1e-30, 8, 7)
    coded = jnp.concatenate([jnp.exp2(gh * (OCT / reach)), jnp.broadcast_to(reach, (META, feats))], axis=0).astype(BF16)
    got = []
    for k in range(2):
        to = (h + k) % 2
        pairs = [(s * nv + t * 2 + h, t * nv + s * 2 + to) for s in range(nt) for t in range(nt)]
        got.append(lax.ppermute(coded[:, to * (feats // 2) : (to + 1) * (feats // 2)], ("teacher", "vocab"), pairs))
    return got


def placed(h, got):
    core = lax.rem(lax.axis_index("vocab"), 2)
    return decoded(jnp.where(core == h, got[0], got[1]))


def weight_kernel(grads, features, *refs):
    refs[-1][...] = jnp.dot(grads[...], features[...], preferred_element_type=F32)


def weight_rows(grads, features, filled, which):
    width, tok = grads.shape
    feats = features.shape[1]
    part = width // TURNS

    def rows(i):
        return which * STEPS + i, 0

    return pl.pallas_call(
        weight_kernel,
        grid=(STEPS,),
        out_shape=jax.ShapeDtypeStruct((width, feats), F32),
        in_specs=[pl.BlockSpec((part, tok), rows), pl.BlockSpec((tok, feats), lambda i: (0, 0))]
        + [pl.BlockSpec(memory_space=pl.ANY)] * len(filled),
        out_specs=pl.BlockSpec((part, feats), rows),
        input_output_aliases={2: 0} if filled else {},
        compiler_params=pltpu.CompilerParams(vmem_limit_bytes=60 * 2**20),
        cost_estimate=pl.CostEstimate(flops=width * tok * feats, bytes_accessed=3 * width * feats, transcendentals=0),
        name="weight",
    )(grads, features, *filled)


def fused(nt, nv, tok, teacher_hidden, teacher_head, student_hidden, student_head):
    head, shead = teacher_head[0].T, student_head.T
    logits, stat, slog, columns = forward(teacher_hidden[0], head, student_hidden, shead, nv, 0)
    gradl, kl = combine(logits, stat, slog, nv, 1)
    every, gh, away, first, loss = gather(gradl, kl, shead, nv, 2)
    chips = nv // 2
    chip = lax.axis_index("vocab") // 2

    def other(a, k):
        return lax.dynamic_index_in_dim(a, lax.rem(chip + k, chips), 0, keepdims=False)

    came = []
    for k in range(1, chips):
        came.append(lax.ppermute(other(away, k), "vocab", [(i, (i + 2 * k) % nv) for i in range(1, nv, 2)]))
    grad_weight = weight_rows(every, columns, (), 0)
    came, grad_weight = lax.optimization_barrier((came, grad_weight))
    second = place(nt, nv, functools.reduce(jnp.add, [decoded(x) for x in came], gh), 1)
    grad_weight = weight_rows(every, columns, (grad_weight,), 1)
    second, grad_weight = lax.optimization_barrier((second, grad_weight))
    grad_hidden = jnp.concatenate([decoded(first), placed(1, second)], axis=0)
    return jnp.sum(loss[0]) / tok, grad_hidden, grad_weight.T


def fits(nt, nv, tok, width):
    own = tok // nt
    return nt == 4 and nv == 2 * nt and own % 256 == 0 and width % (TURNS * META) == 0


def solution(mesh):
    nt, nv = mesh.shape["teacher"], mesh.shape["vocab"]

    def whole(teacher_hidden, teacher_head, student_hidden, student_head):
        tok = student_hidden.shape[0]
        step = fused if fits(nt, nv, tok, student_head.shape[1] // nv) else per_device
        return jax.shard_map(
            lambda *a: step(nt, nv, tok, *a),
            mesh=mesh,
            in_specs=(
                P("teacher", "vocab", None),
                P("teacher", None, "vocab"),
                P("teacher", None),
                P("teacher", "vocab"),
            ),
            out_specs=(P(), P("teacher", "vocab"), P("teacher", "vocab")),
            check_vma=False,
        )(teacher_hidden, teacher_head, student_hidden, student_head)

    return whole
```
